256 devices in a mesh: cells: 64 (over x, z, core), vecs: 4 (over y).
Axes of the slice: x: 4, y: 4, z: 8, core: 2. Of those that a mesh axis runs over, the one named last changes fastest.
Arguments:
- wave_block: float32 [64, 589824], P('vecs', 'cells'), may hold values from -6 to 6
- connectivity: int32 [125, 8192], P(None, 'cells'), may hold values from 0 to 10304, as said below
- send_list: int32 [69696], P('cells'), may hold values from 0 to 9215, as said below
- levels: int32 [8192], P('cells'), may hold values from 0 to 2
- live_cells: int32 [64], P('cells'), may hold values from 64 to 128, as said below
- potential: float32 [125, 8192], P(None, 'cells'), may hold values from -24 to 8
- mass_scale: float32 [589824], P('cells'), may hold values from 0.5 to 2
- center: float32 [], replicated, may hold values from 20 to 30
- halfwidth: float32 [], replicated, may hold values from 25 to 35
- earlier_vectors: bfloat16 [2048, 589824], P(None, ('cells', 'vecs')), may hold values from -0.0078125 to 0.0078125
Outputs:
- filtered: float32 [64, 589824], P(None, ('cells', 'vecs'))
- projections: float32 [2048, 64], P(('cells', 'vecs'))
The draws below stay inside these ranges and needn't reach their ends.
Inputs may be any that keep to these rules, and one draw needn't show every extreme that they name: `connectivity`: column c names the slots of cell c's 125 nodes on its device, node (a,b,c) of the reference cube at row 25 a + 5 b + c. A device's cells form a structured block of 8 x 8 x 2 cells of degree 4 in Morton order, nodes numbered at random over the 9216 node slots; the face of the block toward the device before it lies in the ghost slots 9216 to 10304 in the order of that device's send_list, so that exactly 64 cells of each device name ghost slots. `send_list`: A device's 1089 entries are distinct node slots of its block's face toward the device after it. Cells 0 to live_cells - 1 of a device are in use, the rest of its slots are empty; some device uses all 128, some only 64.
All inputs are finite; a program needn't handle non-finite values.
Results may differ from the reference program's by a relative error of at most 0.0031.
Values may be sent and summed in bfloat16 or wider, within the bound.
No kernel may reach another device: no remote copies, remote signals or barrier semaphores. Data moves between devices by JAX's collectives and lax.ppermute only.
A program may use at most 128 MiB of HBM per device.

```python
import math
import jax
import jax.numpy as jnp
import numpy as np
from jax import lax

NVEC = 64
PREV = 2048
FXY = 8
LZ = 2
CELL_DEV = 128
GHOST = 1089
OWN = 9216
CELLS = 8192
NODES = 589824
N_CELLS = 64


def number_device(device_key):
    return jax.random.permutation(device_key, OWN).astype(jnp.int32)


def mesh_tables(key):
    side_nodes = 4 * FXY + 1
    face_nodes = side_nodes * side_nodes
    layer_nodes = 4 * LZ
    grid_x, grid_y, grid_z = np.meshgrid(np.arange(FXY), np.arange(FXY), np.arange(LZ), indexing='ij')
    grid_x = grid_x.reshape(-1)
    grid_y = grid_y.reshape(-1)
    grid_z = grid_z.reshape(-1)
    morton_codes = np.zeros(grid_x.shape, dtype=grid_x.dtype)
    for bit_index in range(8):
        morton_codes = morton_codes | (grid_x >> bit_index & 1) << 3 * bit_index | (grid_y >> bit_index & 1) << 3 * bit_index + 1 | (grid_z >> bit_index & 1) << 3 * bit_index + 2
    morton_rank = np.argsort(morton_codes, kind='stable')
    local_a, local_b, local_c = np.meshgrid(np.arange(5), np.arange(5), np.arange(5), indexing='ij')
    local_a = local_a.reshape(-1)
    local_b = local_b.reshape(-1)
    local_c = local_c.reshape(-1)
    node_x = 4 * grid_x[morton_rank][None, :] + local_a[:, None]
    node_y = 4 * grid_y[morton_rank][None, :] + local_b[:, None]
    node_z = 4 * grid_z[morton_rank][None, :] + local_c[:, None]
    planar = node_x * side_nodes + node_y
    structured = np.where(node_z == 0, OWN + planar, (node_z - 1) * face_nodes + planar)
    device_keys = jax.random.split(jax.random.fold_in(key, 11), N_CELLS)
    numbering = jax.vmap(number_device)(device_keys)
    table = jnp.asarray(structured, jnp.int32)
    relabelled = jnp.where(table[None] >= OWN, table[None], numbering[:, jnp.minimum(table, OWN - 1)])
    top_face = numbering[:, (layer_nodes - 1) * face_nodes + jnp.arange(face_nodes, dtype=jnp.int32)]
    return (relabelled.astype(jnp.int32), top_face.astype(jnp.int32))


def draw_connectivity(key, part):
    relabelled, top_face = mesh_tables(key)
    return relabelled.transpose(1, 0, 2).reshape(125, CELLS)


def draw_send_list(key, part):
    relabelled, top_face = mesh_tables(key)
    return top_face.reshape(GHOST * N_CELLS)


def draw_live_cells(key, part):
    counts_drawn = jax.random.randint(jax.random.fold_in(key, 3), (N_CELLS,), CELL_DEV // 2, CELL_DEV + 1)
    device_rank = jax.random.permutation(jax.random.fold_in(key, 5), N_CELLS)
    counts_drawn = counts_drawn.at[device_rank[0]].set(CELL_DEV)
    counts_drawn = counts_drawn.at[device_rank[1]].set(CELL_DEV // 2)
    return counts_drawn.astype(jnp.int32)


def touch_ends(result, key, least, largest):
    spot = [jax.random.randint(jax.random.fold_in(key, axis), (), 0, length) for axis, length in enumerate(result.shape)]
    longest = result.shape.index(max(result.shape))
    next_to = spot[:longest] + [(spot[longest] + 1) % result.shape[longest]] + spot[longest + 1:]
    return result.at[tuple(spot)].set(least).at[tuple(next_to)].set(largest)


def level_of(stream_key, shape, cuts, smallest, top_value):
    def one(axis_at, shards_of):
        heights = jax.random.uniform(jax.random.fold_in(jax.random.fold_in(stream_key, 6), axis_at), (shards_of,), jnp.float32, smallest / len(cuts), top_value / len(cuts))
        return jnp.repeat(jnp.exp(heights), shape[axis_at] // shards_of).reshape((-1,) + (1,) * (len(shape) - axis_at - 1))

    gain = one(*cuts[0])
    for cut in cuts[1:]:
        gain = gain * one(*cut)
    return gain


def gaussian(own_key, shape, spread, most, cuts=(), kind=jnp.bfloat16):
    values = jax.random.normal(own_key, shape, jnp.float32) * spread
    if len(cuts) > 0:
        values = level_of(own_key, shape, cuts, -0.22, 0.18) * values
    return jnp.clip(values, min=-most, max=most).astype(kind)


def setup_inputs(seed: int = 0) -> dict:
    splits = jax.random.split(jax.random.key(seed), 11)
    return {
        "wave_block": gaussian(splits[0], (NVEC, NODES), 1.0, 6.0, ((0, 4), (1, 64)), jnp.float32),
        "connectivity": draw_connectivity(jax.random.fold_in(splits[10], 71), 0),
        "send_list": draw_send_list(jax.random.fold_in(splits[10], 71), 0),
        "levels": touch_ends(jax.random.randint(splits[3], (CELLS,), 0, 3), jax.random.fold_in(splits[3], 1), 0, 2).astype(jnp.int32),
        "live_cells": draw_live_cells(jax.random.fold_in(splits[10], 71), 0),
        "potential": jnp.clip(-24.0 + 32.0 * jax.random.uniform(splits[5], (125, CELLS), jnp.float32) ** level_of(splits[5], (125, CELLS), ((1, 64),), -0.2, 0.2), -24.0, 8.0),
        "mass_scale": jnp.clip(jnp.exp(math.log(2.0) - 1.3862944 * jax.random.uniform(splits[6], (NODES,), jnp.float32) ** level_of(splits[6], (NODES,), ((0, 64),), -0.2, 0.2)), 0.5, 2.0),
        "center": jnp.clip(jax.random.uniform(splits[7], (), jnp.float32, 20.0, 30.0), 20.0, 30.0),
        "halfwidth": jnp.clip(jax.random.uniform(splits[8], (), jnp.float32, 25.0, 35.0), 25.0, 35.0),
        "earlier_vectors": gaussian(splits[9], (PREV, NODES), NODES ** -0.5, 0.0078125, ((1, 256),)),
    }


def gll_tables():
    root_value = math.sqrt(3.0 / 7.0)
    points = np.array([-1.0, -root_value, 0.0, root_value, 1.0])
    weights = np.array([0.1, 49.0 / 90.0, 32.0 / 45.0, 49.0 / 90.0, 0.1])
    barycentric = np.ones(5)
    for node_index in range(5):
        for other_node in range(5):
            if other_node != node_index:
                barycentric[node_index] = barycentric[node_index] / (points[node_index] - points[other_node])
    derivative = np.zeros((5, 5))
    for row_index in range(5):
        for col_index in range(5):
            if row_index != col_index:
                derivative[row_index, col_index] = barycentric[col_index] / barycentric[row_index] / (points[row_index] - points[col_index])
        derivative[row_index, row_index] = -np.sum(derivative[row_index])
    mass_one = np.zeros((5, 5))
    for node_index in range(5):
        mass_one[node_index, node_index] = weights[node_index]
    laplace_one = derivative.T @ mass_one @ derivative
    stiffness = np.kron(np.kron(laplace_one, mass_one), mass_one) + np.kron(np.kron(mass_one, laplace_one), mass_one) + np.kron(np.kron(mass_one, mass_one), laplace_one)
    quadrature = np.kron(np.kron(weights, weights), weights)
    return (stiffness.astype(np.float32), quadrature.astype(np.float32))

def reference(wave_block, connectivity, send_list, levels, live_cells, potential, mass_scale, center, halfwidth, earlier_vectors):
    stiffness, quadrature = gll_tables()
    stiffness_low = jnp.asarray(stiffness).astype(jnp.bfloat16)
    quad_weights = jnp.asarray(quadrature).astype(jnp.float32)
    conn_dev = connectivity.reshape(125, N_CELLS, CELL_DEV).transpose(1, 0, 2)
    pot_dev = potential.reshape(125, N_CELLS, CELL_DEV).transpose(1, 0, 2)
    send_dev = send_list.reshape(N_CELLS, GHOST)
    cell_size = jnp.exp2(-levels.astype(jnp.float32)).reshape(N_CELLS, CELL_DEV)
    in_use = (jnp.arange(CELL_DEV, dtype=jnp.int32)[None, :] < live_cells[:, None]).astype(jnp.float32)
    kinetic = cell_size / 4.0 * in_use
    volume = cell_size ** 3 / 8.0 * in_use
    coefficient = volume[:, None, :] * quad_weights[None, :, None] * pot_dev

    def cell_sum(inputs):
        extended, cells_conn, kin_part, coeff_part = inputs
        values = extended[:, cells_conn].astype(jnp.bfloat16)
        stiff_part = jnp.einsum('jk,vkc->vjc', stiffness_low.astype(jnp.float32), values.astype(jnp.float32))
        cell_terms = kin_part[None, None, :] * stiff_part + coeff_part[None] * values.astype(jnp.float32)
        return jnp.zeros((NVEC, OWN + GHOST), jnp.float32).at[:, cells_conn].add(cell_terms)

    def take_face(vectors, slots):
        return vectors[:, slots]

    def add_back(sums, returned, slots):
        return sums[:, :OWN].at[:, slots].add(returned)

    def apply_operator(vectors):
        scaled = vectors * mass_scale[None, :]
        per_dev = scaled.reshape(NVEC, N_CELLS, OWN).transpose(1, 0, 2)
        top_faces = jax.vmap(take_face)(per_dev, send_dev)
        ghosts = jnp.concatenate([jnp.zeros((1, NVEC, GHOST), jnp.float32), top_faces[:-1]], 0)
        extended = jnp.concatenate([per_dev, ghosts], 2)
        slot_sums = lax.map(cell_sum, (extended, conn_dev, kinetic, coefficient))
        returned = jnp.concatenate([slot_sums[1:, :, OWN:], jnp.zeros((1, NVEC, GHOST), jnp.float32)], 0)
        owned = jax.vmap(add_back)(slot_sums, returned, send_dev)
        return owned.transpose(1, 0, 2).reshape(NVEC, NODES) * mass_scale[None, :]
    degree_one = (apply_operator(wave_block) - center * wave_block) / halfwidth
    degree_two = 2.0 * (apply_operator(degree_one) - center * degree_one) / halfwidth - wave_block
    rounded = degree_two.astype(jnp.bfloat16)
    projections = jnp.dot(earlier_vectors, rounded.T, preferred_element_type=jnp.float32)
    projection_low = projections.astype(jnp.bfloat16)
    filtered = rounded.astype(jnp.float32) - jnp.dot(projection_low.T, earlier_vectors, preferred_element_type=jnp.float32)
    return (filtered, projections)
```

```python
import math

import jax
import jax.numpy as jnp
import numpy as np
from jax import lax
from jax.experimental import pallas as pl
from jax.experimental.pallas import tpu as pltpu
from jax.sharding import PartitionSpec as P

F32, BF16, I32 = jnp.float32, jnp.bfloat16, jnp.int32
AXES = ("cells", "vecs")
LANES = 128
VMEM_LIMIT = 48 * 2**20


def gll_tables():
    root_value = math.sqrt(3.0 / 7.0)
    points = np.array([-1.0, -root_value, 0.0, root_value, 1.0])
    weights = np.array([0.1, 49.0 / 90.0, 32.0 / 45.0, 49.0 / 90.0, 0.1])
    barycentric = np.ones(5)
    for node_index in range(5):
        for other_node in range(5):
            if other_node != node_index:
                barycentric[node_index] = barycentric[node_index] / (
                    points[node_index] - points[other_node]
                )
    derivative = np.zeros((5, 5))
    for row_index in range(5):
        for col_index in range(5):
            if row_index != col_index:
                derivative[row_index, col_index] = (
                    barycentric[col_index]
                    / barycentric[row_index]
                    / (points[row_index] - points[col_index])
                )
        derivative[row_index, row_index] = -np.sum(derivative[row_index])
    mass_one = np.zeros((5, 5))
    for node_index in range(5):
        mass_one[node_index, node_index] = weights[node_index]
    laplace_one = derivative.T @ mass_one @ derivative
    stiffness = (
        np.kron(np.kron(laplace_one, mass_one), mass_one)
        + np.kron(np.kron(mass_one, laplace_one), mass_one)
        + np.kron(np.kron(mass_one, mass_one), laplace_one)
    )
    quadrature = np.kron(np.kron(weights, weights), weights)
    return (stiffness.astype(np.float32), quadrature.astype(np.float32))


STIFFNESS, QUADRATURE = gll_tables()
STIFFNESS = STIFFNESS.astype(jnp.bfloat16).astype(np.float32)


def node(a, b, c):
    return 25 * a + 5 * b + c


def lane_index(rows):
    return lax.broadcasted_iota(I32, (rows, LANES), 1)


def axis_bits(lane, axis):
    return [(lane >> bit) & 1 for bit in ((0, 3, 5), (1, 4, 6))[axis]]


def axis_place(lane, axis):
    low, mid, high = axis_bits(lane, axis)
    return low + 2 * mid + 4 * high


def below_of(lane, axis):
    low, mid, high = axis_bits(lane, axis)
    scale = 1 + axis
    step = jnp.where(low == 1, 1, jnp.where(mid == 1, 7, 23)) * scale
    first = axis_place(lane, axis) == 0
    return jnp.where(first, lane, lane - step), jnp.logical_not(first)


def above_of(lane, axis):
    low, mid, high = axis_bits(lane, axis)
    scale = 1 + axis
    step = jnp.where(low == 0, 1, jnp.where(mid == 0, 7, 23)) * scale
    last = axis_place(lane, axis) == 7
    return jnp.where(last, lane, lane + step), jnp.logical_not(last)


def pick(values, index):
    return jnp.take_along_axis(values, index, axis=1)


def up_layer(values):
    return pltpu.roll(values, 4, 1)


def down_layer(values):
    return pltpu.roll(values, LANES - 4, 1)


def row_groups(values, group):
    return values.shape[0] // group


def split_low(values):
    high = values.astype(BF16)
    return high, (values - high.astype(F32)).astype(BF16)


def gather_kernel(vectors, conn_ref, wave_ref, mass_ref, wave_out, mass_out, face_out, table):
    groups = wave_ref.shape[1] // 256
    rows = vectors * groups
    high, low = split_low(wave_ref[...])
    for h in range(groups):
        table[vectors * h : vectors * (h + 1), 0:256] = high[:, 256 * h : 256 * (h + 1)]
        table[vectors * h : vectors * (h + 1), 256:512] = low[:, 256 * h : 256 * (h + 1)]
    mass_high, mass_low = split_low(mass_ref[...])
    table[rows : rows + groups, 0:256] = mass_high
    table[rows : rows + groups, 256:512] = mass_low
    width = 4 * LANES
    place = lax.broadcasted_iota(I32, (256, width), 0).astype(F32).astype(BF16)
    group_row = lax.broadcasted_iota(I32, (groups, width), 0)

    def one(ab, carry):
        slots = jnp.concatenate([conn_ref[pl.ds(5 * ab + c, 1), :] for c in range(1, 5)], 1)
        within = jnp.broadcast_to((slots & 255).astype(F32).astype(BF16), (256, width))
        chosen = jnp.where(place == within, BF16(1), BF16(0))
        found = jnp.dot(
            table[...], jnp.concatenate([chosen, chosen], 0), preferred_element_type=F32
        )
        group = slots >> 8
        wide = jnp.broadcast_to(group, (vectors, width))
        total = jnp.zeros((vectors, width), F32)
        for h in range(groups):
            total = jnp.where(wide == h, found[vectors * h : vectors * (h + 1)], total)
        mass = jnp.sum(
            jnp.where(
                group_row == jnp.broadcast_to(group, (groups, width)),
                found[rows : rows + groups],
                0.0,
            ),
            0,
            keepdims=True,
        )
        for c in range(1, 5):
            wave_out[5 * ab + c] = total[:, LANES * (c - 1) : LANES * c]
            mass_out[pl.ds(5 * ab + c, 1), :] = mass[:, LANES * (c - 1) : LANES * c]
        return carry

    lax.fori_loop(0, 25, one, 0, unroll=5)
    upper = (lane_index(vectors) >> 2) & 1 == 1
    upper_one = (lane_index(1) >> 2) & 1 == 1
    for i in range(13):
        first = wave_out[5 * (2 * i) + 4]
        first_mass = mass_out[5 * (2 * i) + 4 : 5 * (2 * i) + 5, :]
        second, second_mass = first, first_mass
        if i < 12:
            second = wave_out[5 * (2 * i + 1) + 4]
            second_mass = mass_out[5 * (2 * i + 1) + 4 : 5 * (2 * i + 1) + 5, :]
        face_out[i, 0:vectors, :] = jnp.where(upper, first, down_layer(second))
        packed = jnp.where(upper_one, first_mass, down_layer(second_mass))
        face_out[i, vectors : vectors + 8, :] = jnp.broadcast_to(packed, (8, LANES))


def apply_cells(values, terms, potential_ref, levels_ref, live_ref, vectors):
    lane = lane_index(1)
    size = jnp.exp2(-levels_ref[...].astype(F32))
    in_use = jnp.where(lane < live_ref[0], 1.0, 0.0).astype(F32)
    kinetic_row = size / 4.0 * in_use
    volume_row = size * size * size / 8.0 * in_use
    kinetic = jnp.broadcast_to(kinetic_row, (8, LANES))

    def one(t, carry):
        part = pl.ds(pl.multiple_of(8 * t, 8), 8)
        for j in range(125):
            total = None
            for k in np.flatnonzero(STIFFNESS[j]):
                term = values[int(k), part, :] * float(STIFFNESS[j, k])
                total = term if total is None else total + term
            weight = volume_row * float(QUADRATURE[j]) * potential_ref[j : j + 1, :]
            weight = jnp.broadcast_to(weight, (8, LANES))
            terms[j, part, :] = kinetic * total + weight * values[j, part, :]
        return carry

    lax.fori_loop(0, vectors // 8, one, 0)


def join_cells(terms, vectors):
    lane = lane_index(8)
    upper = (lane >> 2) & 1 == 1

    def one(t, carry):
        part = pl.ds(pl.multiple_of(8 * t, 8), 8)
        for axis in range(2):
            before, has_before = below_of(lane, axis)
            after, has_after = above_of(lane, axis)
            for other in range(5):
                for c in range(5):
                    start = node(0, other, c) if axis == 0 else node(other, 0, c)
                    end = node(4, other, c) if axis == 0 else node(other, 4, c)
                    first, last = terms[start, part, :], terms[end, part, :]
                    joined = first + jnp.where(has_before, pick(last, before), 0.0)
                    terms[start, part, :] = joined
                    terms[end, part, :] = jnp.where(has_after, pick(joined, after), last)
        for ab in range(25):
            first, last = terms[5 * ab, part, :], terms[5 * ab + 4, part, :]
            joined = first + jnp.where(upper, up_layer(last), 0.0)
            terms[5 * ab, part, :] = joined
            terms[5 * ab + 4, part, :] = jnp.where(upper, last, down_layer(joined))
        return carry

    lax.fori_loop(0, vectors // 8, one, 0)


def pack_lower(terms, face_out, vectors):
    upper = (lane_index(vectors) >> 2) & 1 == 1
    for i in range(13):
        first = terms[5 * (2 * i)]
        second = terms[5 * (2 * i + 1)] if i < 12 else first
        face_out[i] = jnp.where(upper, up_layer(second), first).astype(BF16)


def pack_upper(terms, face_out, vectors):
    upper = (lane_index(vectors) >> 2) & 1 == 1
    for i in range(13):
        first = terms[5 * (2 * i) + 4]
        second = terms[5 * (2 * i + 1) + 4] if i < 12 else first
        face_out[i] = jnp.where(upper, first, down_layer(second)).astype(BF16)


def from_below(packed, ab):
    return packed if ab % 2 == 1 else down_layer(packed)


def from_above(packed, ab):
    return packed if ab % 2 == 1 else up_layer(packed)


def first_kernel(
    vectors, wave_ref, mass_ref, ghost_ref, potential_ref, levels_ref, live_ref,
    terms, low_wave, low_mass, face_down, face_up, values,
):
    upper = (lane_index(vectors) >> 2) & 1 == 1
    upper_one = (lane_index(1) >> 2) & 1 == 1
    for ab in range(25):
        packed = ghost_ref[ab // 2]
        wave = jnp.where(
            upper, up_layer(wave_ref[5 * ab + 4]), from_below(packed[0:vectors], ab)
        )
        mass = jnp.where(
            upper_one,
            up_layer(mass_ref[5 * ab + 4 : 5 * ab + 5, :]),
            from_below(packed[vectors : vectors + 1], ab),
        )
        low_wave[ab] = wave
        low_mass[ab : ab + 1, :] = mass
        values[5 * ab] = (wave * mass).astype(BF16).astype(F32)
        for c in range(1, 5):
            j = 5 * ab + c
            values[j] = (wave_ref[j] * mass_ref[j : j + 1, :]).astype(BF16).astype(F32)
    apply_cells(values, terms, potential_ref, levels_ref, live_ref, vectors)
    join_cells(terms, vectors)
    pack_lower(terms, face_down, vectors)
    pack_upper(terms, face_up, vectors)


def second_kernel(
    vectors, sums_ref, wave_ref, mass_ref, low_wave, low_mass, above_ref, below_ref,
    potential_ref, levels_ref, live_ref, scalars_ref, result, face_down, values, terms,
):
    upper = (lane_index(vectors) >> 2) & 1 == 1
    center, inverse = scalars_ref[0], scalars_ref[1]
    for ab in range(25):
        for c in range(5):
            j = 5 * ab + c
            total = sums_ref[j]
            if c == 0:
                below = from_below(below_ref[ab // 2].astype(F32), ab)
                total = total + jnp.where(upper, 0.0, below)
                wave, mass = low_wave[ab], low_mass[ab : ab + 1, :]
            else:
                wave, mass = wave_ref[j], mass_ref[j : j + 1, :]
            if c == 4:
                above = from_above(above_ref[ab // 2].astype(F32), ab)
                total = total + jnp.where(upper, above, 0.0)
            one = (mass * total - center * wave) * inverse
            values[j] = (one * mass).astype(BF16).astype(F32)
            result[j] = -2.0 * center * inverse * one - wave
    apply_cells(values, terms, potential_ref, levels_ref, live_ref, vectors)
    join_cells(terms, vectors)
    pack_lower(terms, face_down, vectors)
    for ab in range(25):
        for c in range(1, 5):
            j = 5 * ab + c
            result[j] = result[j] + (2.0 * inverse) * mass_ref[j : j + 1, :] * terms[j]


def scatter_kernel(
    vectors, conn_ref, result_ref, mass_ref, above_ref, wave_ref, scalars_ref, out_ref, total
):
    groups = wave_ref.shape[1] // 256
    rows = vectors * groups
    center, inverse = scalars_ref[0], scalars_ref[1]
    width = 4 * LANES
    place = lax.broadcasted_iota(I32, (256, width), 0).astype(F32).astype(BF16)
    group_row = lax.broadcasted_iota(I32, (groups, width), 0)
    lane = lane_index(1)
    last_x, last_y = axis_place(lane, 0) == 7, axis_place(lane, 1) == 7
    upper = (lane_index(vectors) >> 2) & 1 == 1
    total[...] = jnp.zeros_like(total)
    for ab in range(25):
        keep = None
        if ab // 5 == 4:
            keep = last_x
        if ab % 5 == 4:
            keep = last_y if keep is None else jnp.logical_and(keep, last_y)
        pieces, slots = [], []
        for c in range(1, 5):
            j = 5 * ab + c
            value = result_ref[j]
            if c == 4:
                above = from_above(above_ref[ab // 2].astype(F32), ab)
                share = (2.0 * inverse) * mass_ref[j : j + 1, :] * above
                value = value + jnp.where(upper, share, 0.0)
            pieces.append(value.astype(BF16))
            slot = conn_ref[j : j + 1, :]
            slots.append(slot if keep is None else jnp.where(keep, slot, 65535))
        value = jnp.concatenate(pieces, 1)
        slot = jnp.concatenate(slots, 1)
        within = jnp.broadcast_to((slot & 255).astype(F32).astype(BF16), (256, width))
        chosen = jnp.where(place == within, BF16(1), BF16(0))
        group = slot >> 8
        wide = jnp.broadcast_to(group.astype(F32).astype(BF16), (vectors, width))
        spread = [jnp.where(wide == BF16(h), value, BF16(0)) for h in range(groups)]
        held = jnp.where(group_row == jnp.broadcast_to(group, (groups, width)), 1.0, 0.0)
        spread.append(jnp.concatenate([held, jnp.zeros((48 - groups, width), F32)], 0).astype(BF16))
        total[...] += lax.dot_general(
            jnp.concatenate(spread, 0),
            chosen,
            (((1,), (1,)), ((), ())),
            preferred_element_type=F32,
        )
    quarter = groups // out_ref.shape[0]
    for h in range(groups):
        wave = wave_ref[:, 256 * h : 256 * (h + 1)]
        one = -center * wave * inverse
        alone = -2.0 * center * one * inverse - wave
        used = total[rows + h : rows + h + 1, :] > 0.5
        value = jnp.where(used, total[vectors * h : vectors * (h + 1), :], alone)
        at = h % quarter
        out_ref[h // quarter, :, 256 * at : 256 * (at + 1)] = value.astype(BF16)


VMEM_SPEC = pl.BlockSpec(memory_space=pltpu.VMEM)
SMEM_SPEC = pl.BlockSpec(memory_space=pltpu.SMEM)


def call(kernel, name, out_shape, specs, scratch, *operands):
    return pl.pallas_call(
        kernel,
        out_shape=out_shape,
        in_specs=specs,
        out_specs=jax.tree.map(lambda _: VMEM_SPEC, out_shape),
        scratch_shapes=scratch,
        compiler_params=pltpu.CompilerParams(vmem_limit_bytes=VMEM_LIMIT),
        name=name,
    )(*operands)


def passed_along(value, axis, steps):
    count = lax.axis_size(axis)
    leading, last = (max(0, -steps), min(count, count - steps))
    return lax.ppermute(value, axis, [(source, source + steps) for source in range(leading, last)])


def per_device(
    wave_block, connectivity, send_list, levels, live_cells, potential, mass_scale,
    center, halfwidth, earlier_vectors,
):
    vectors, owned = wave_block.shape
    groups = owned // 256
    table_rows = vectors * groups + 48
    scalars = jnp.stack([center, 1.0 / halfwidth])
    level_row = levels.reshape(1, LANES)
    shape = jax.ShapeDtypeStruct
    full = (125, vectors, LANES)
    wave, mass, face = call(
        lambda *refs: gather_kernel(vectors, *refs),
        "gather_nodes",
        (shape(full, F32), shape((125, LANES), F32), shape((13, vectors + 8, LANES), F32)),
        [VMEM_SPEC] * 3,
        [pltpu.VMEM((table_rows, 512), BF16)],
        connectivity, wave_block, mass_scale.reshape(groups, 256),
    )
    ghost = passed_along(face, "cells", 1)
    packed = shape((13, vectors, LANES), BF16)
    sums, low_wave, low_mass, face_down, face_up = call(
        lambda *refs: first_kernel(vectors, *refs),
        "first_operator",
        (shape(full, F32), shape((25, vectors, LANES), F32), shape((25, LANES), F32), packed, packed),
        [VMEM_SPEC] * 5 + [SMEM_SPEC],
        [pltpu.VMEM(full, F32)],
        wave, mass, ghost, potential, level_row, live_cells,
    )
    above = passed_along(face_down, "cells", -1)
    below = passed_along(face_up, "cells", 1)
    result, face_down = call(
        lambda *refs: second_kernel(vectors, *refs),
        "second_operator",
        (shape(full, F32), packed),
        [VMEM_SPEC] * 9 + [SMEM_SPEC] * 2,
        [pltpu.VMEM(full, F32), pltpu.VMEM(full, F32)],
        sums, wave, mass, low_wave, low_mass, above, below, potential, level_row, live_cells, scalars,
    )
    above = passed_along(face_down, "cells", -1)
    parts = lax.axis_size("vecs")
    rounded = call(
        lambda *refs: scatter_kernel(vectors, *refs),
        "scatter_nodes",
        shape((parts, vectors, owned // parts), BF16),
        [VMEM_SPEC] * 5 + [SMEM_SPEC],
        [pltpu.VMEM((table_rows, 256), F32)],
        connectivity, result, mass, above, wave_block, scalars,
    )
    quarter = lax.all_to_all(rounded, "vecs", split_axis=0, concat_axis=0, tiled=True)
    quarter = quarter.reshape(parts * vectors, owned // parts)
    devices = lax.axis_size(AXES)
    total_vectors = parts * vectors
    row_share = earlier_vectors.shape[0] // devices
    partial_sum = lax.dot_general(
        earlier_vectors, quarter, (((1,), (1,)), ((), ())), preferred_element_type=F32
    )
    half = row_share // 2
    partial_sum = partial_sum.reshape(devices, 2, half, total_vectors).transpose(0, 2, 1, 3)
    partial_sum = partial_sum.reshape(devices * half, 2 * total_vectors)
    shares = lax.all_to_all(partial_sum, AXES, split_axis=0, concat_axis=0, tiled=True)
    own = jnp.sum(shares.reshape(devices, half, 2 * total_vectors), 0)
    own_rows = own.reshape(half, 2, total_vectors).transpose(1, 0, 2).reshape(row_share, total_vectors)
    low = jnp.broadcast_to(own.astype(BF16)[None], (devices, half, 2 * total_vectors))
    low = lax.all_to_all(low, AXES, split_axis=0, concat_axis=0, tiled=True)
    low = low.reshape(devices, half, 2, total_vectors).transpose(0, 2, 1, 3)
    low = low.reshape(devices * row_share, total_vectors)
    filtered = quarter.astype(F32) - lax.dot_general(
        low, earlier_vectors, (((0,), (0,)), ((), ())), preferred_element_type=F32
    )
    return (filtered, own_rows)


def solution(mesh):
    in_specs = (
        P("vecs", "cells"),
        P(None, "cells"),
        P("cells"),
        P("cells"),
        P("cells"),
        P(None, "cells"),
        P("cells"),
        P(),
        P(),
        P(None, AXES),
    )
    out_specs = (P(None, AXES), P(AXES, None))
    return jax.shard_map(
        per_device, mesh=mesh, in_specs=in_specs, out_specs=out_specs, check_vma=False
    )
```

```python
import math

import jax
import jax.numpy as jnp
import numpy as np
from jax import lax
from jax.experimental import pallas as pl
from jax.experimental.pallas import tpu as pltpu
from jax.sharding import PartitionSpec as P

F32, BF16, I32 = jnp.float32, jnp.bfloat16, jnp.int32
AXES = ("cells", "vecs")
LANES = 128
VMEM_LIMIT = 20 * 2**20


def gll_tables():
    root_value = math.sqrt(3.0 / 7.0)
    points = np.array([-1.0, -root_value, 0.0, root_value, 1.0])
    weights = np.array([0.1, 49.0 / 90.0, 32.0 / 45.0, 49.0 / 90.0, 0.1])
    barycentric = np.ones(5)
    for node_index in range(5):
        for other_node in range(5):
            if other_node != node_index:
                barycentric[node_index] = barycentric[node_index] / (
                    points[node_index] - points[other_node]
                )
    derivative = np.zeros((5, 5))
    for row_index in range(5):
        for col_index in range(5):
            if row_index != col_index:
                derivative[row_index, col_index] = (
                    barycentric[col_index]
                    / barycentric[row_index]
                    / (points[row_index] - points[col_index])
                )
        derivative[row_index, row_index] = -np.sum(derivative[row_index])
    mass_one = np.zeros((5, 5))
    for node_index in range(5):
        mass_one[node_index, node_index] = weights[node_index]
    laplace_one = derivative.T @ mass_one @ derivative
    stiffness = (
        np.kron(np.kron(laplace_one, mass_one), mass_one)
        + np.kron(np.kron(mass_one, laplace_one), mass_one)
        + np.kron(np.kron(mass_one, mass_one), laplace_one)
    )
    quadrature = np.kron(np.kron(weights, weights), weights)
    return (stiffness.astype(np.float32), quadrature.astype(np.float32))


STIFFNESS, QUADRATURE = gll_tables()
STIFFNESS = STIFFNESS.astype(jnp.bfloat16).astype(np.float32)


def node(a, b, c):
    return 25 * a + 5 * b + c


def lane_index(rows):
    return lax.broadcasted_iota(I32, (rows, LANES), 1)


def axis_bits(lane, axis):
    return [(lane >> bit) & 1 for bit in ((0, 3, 5), (1, 4, 6))[axis]]


def axis_place(lane, axis):
    low, mid, high = axis_bits(lane, axis)
    return low + 2 * mid + 4 * high


def below_of(lane, axis):
    low, mid, high = axis_bits(lane, axis)
    scale = 1 + axis
    step = jnp.where(low == 1, 1, jnp.where(mid == 1, 7, 23)) * scale
    first = axis_place(lane, axis) == 0
    return jnp.where(first, lane, lane - step), jnp.logical_not(first)


def above_of(lane, axis):
    low, mid, high = axis_bits(lane, axis)
    scale = 1 + axis
    step = jnp.where(low == 0, 1, jnp.where(mid == 0, 7, 23)) * scale
    last = axis_place(lane, axis) == 7
    return jnp.where(last, lane, lane + step), jnp.logical_not(last)


def pick(values, index):
    return jnp.take_along_axis(values, index, axis=1)


def up_layer(values):
    return pltpu.roll(values, 4, 1)


def down_layer(values):
    return pltpu.roll(values, LANES - 4, 1)


def split_low(values):
    high = values.astype(BF16)
    return high, (values - high.astype(F32)).astype(BF16)


class Nodes:
    def __init__(self, low, mid, top):
        self.low, self.mid, self.top = low, mid, top

    def at(self, j):
        ab, c = divmod(j, 5)
        if c == 0:
            return self.low, ab
        if c == 4:
            return self.top, ab
        return self.mid, 3 * ab + c - 1

    def load(self, j, part=slice(None)):
        ref, row = self.at(j)
        return ref[row, part, :]

    def store(self, j, value, part=slice(None)):
        ref, row = self.at(j)
        ref[row, part, :] = value

    def line(self, j):
        ref, row = self.at(j)
        return ref[row : row + 1, :]

    def store_line(self, j, value):
        ref, row = self.at(j)
        ref[row : row + 1, :] = value


ALL_ROWS = list(range(125))
MID_ROWS = [j for j in ALL_ROWS if j % 5 in (1, 2, 3)]
LOW_ROWS = [j for j in ALL_ROWS if j % 5 == 0]
TOP_ROWS = [j for j in ALL_ROWS if j % 5 == 4]


def upper_lanes(rows):
    return (lane_index(rows) >> 2) & 1 == 1


def one_hot(slots, width):
    place = lax.broadcasted_iota(I32, (256, width), 0).astype(F32).astype(BF16)
    within = jnp.broadcast_to((slots & 255).astype(F32).astype(BF16), (256, width))
    return jnp.where(place == within, BF16(1), BF16(0))


def gather_rows(vectors, groups, rows, conn, table, wave, mass):
    base = vectors * groups
    start = 0
    while start < len(rows):
        count = 5 if len(rows) - start == 5 else min(4, len(rows) - start)
        width = count * LANES
        chunk = rows[start : start + count]
        slots = jnp.concatenate([conn[j : j + 1, :] for j in chunk], 1)
        chosen = one_hot(slots, width)
        found = jnp.dot(
            table[...], jnp.concatenate([chosen, chosen], 0), preferred_element_type=F32
        )
        group = slots >> 8
        wide = jnp.broadcast_to(group, (vectors, width))
        total = jnp.zeros((vectors, width), F32)
        for h in range(groups):
            total = jnp.where(wide == h, found[vectors * h : vectors * (h + 1)], total)
        group_row = lax.broadcasted_iota(I32, (groups, width), 0)
        mine = group_row == jnp.broadcast_to(group, (groups, width))
        line = jnp.sum(jnp.where(mine, found[base : base + groups], 0.0), 0, keepdims=True)
        for i in range(count):
            wave[start + i] = total[:, LANES * i : LANES * (i + 1)]
            mass[start + i : start + i + 1, :] = line[:, LANES * i : LANES * (i + 1)]
        start += count


def gather_face_kernel(
    vectors, conn_hbm, wave_hbm, mass_hbm, table, conn, wave_top, mass_top, face_out,
    wave_in, mass_in, sems,
):
    copies = [
        pltpu.make_async_copy(wave_hbm, wave_in, sems.at[0]),
        pltpu.make_async_copy(mass_hbm, mass_in, sems.at[1]),
        pltpu.make_async_copy(conn_hbm, conn, sems.at[2]),
    ]
    for copy in copies:
        copy.start()
    for copy in copies:
        copy.wait()
    groups = wave_in.shape[1] // 256
    base = vectors * groups
    high, low = split_low(wave_in[...])
    for h in range(groups):
        table[vectors * h : vectors * (h + 1), 0:256] = high[:, 256 * h : 256 * (h + 1)]
        table[vectors * h : vectors * (h + 1), 256:512] = low[:, 256 * h : 256 * (h + 1)]
    for half in range(2):
        high, low = split_low(mass_in[pl.ds(half, groups, stride=2), :])
        spare = jnp.zeros((table.shape[0] - base - groups, LANES), F32)
        columns = slice(LANES * half, LANES * (half + 1))
        table[base:, columns] = jnp.concatenate([high.astype(F32), spare], 0).astype(BF16)
        columns = slice(256 + LANES * half, 256 + LANES * (half + 1))
        table[base:, columns] = jnp.concatenate([low.astype(F32), spare], 0).astype(BF16)
    gather_rows(vectors, groups, TOP_ROWS, conn, table, wave_top, mass_top)
    upper, upper_one = upper_lanes(vectors), upper_lanes(1)
    for i in range(13):
        second = min(2 * i + 1, 24)
        face_out[i, 0:vectors, :] = jnp.where(upper, wave_top[2 * i], down_layer(wave_top[second]))
        packed = jnp.where(
            upper_one,
            mass_top[2 * i : 2 * i + 1, :],
            down_layer(mass_top[second : second + 1, :]),
        )
        face_out[i, vectors : vectors + 8, :] = jnp.broadcast_to(packed, (8, LANES))


def gather_rest_kernel(
    vectors, groups, table, conn, potential_hbm, levels_hbm, live_ref,
    wave_mid, mass_mid, kinetic, coefficient, levels_in, sems,
):
    copies = [
        pltpu.make_async_copy(potential_hbm, coefficient, sems.at[0]),
        pltpu.make_async_copy(levels_hbm, levels_in, sems.at[1]),
    ]
    for copy in copies:
        copy.start()
    gather_rows(vectors, groups, MID_ROWS, conn, table, wave_mid, mass_mid)
    copies[0].wait()
    copies[1].wait()
    size = jnp.exp2(-levels_in[...].astype(F32))
    in_use = jnp.where(lane_index(1) < live_ref[0], 1.0, 0.0).astype(F32)
    kinetic[...] = jnp.broadcast_to(size / 4.0 * in_use, (8, LANES))
    volume = size * size * size / 8.0 * in_use
    for j in ALL_ROWS:
        line = volume * float(QUADRATURE[j]) * coefficient[j : j + 1, :]
        coefficient[j : j + 1, :] = line


def apply_cells(values, terms, kinetic, coefficient, rows, vectors):
    def one(t, carry):
        part = pl.ds(pl.multiple_of(8 * t, 8), 8)
        for j in rows:
            total = None
            for k in np.flatnonzero(STIFFNESS[j]):
                term = values[int(k), part, :] * float(STIFFNESS[j, k])
                total = term if total is None else total + term
            weight = jnp.broadcast_to(coefficient[j : j + 1, :], (8, LANES))
            terms.store(j, kinetic[...] * total + weight * values[j, part, :], part)
        return carry

    lax.fori_loop(0, vectors // 8, one, 0)


def join_layer(terms, layers, vectors):
    lane = lane_index(8)
    moves = [below_of(lane, axis) + above_of(lane, axis) for axis in range(2)]

    def one(t, carry):
        part = pl.ds(pl.multiple_of(8 * t, 8), 8)
        for axis in range(2):
            before, has_before, after, has_after = moves[axis]
            for other in range(5):
                for c in layers:
                    start = node(0, other, c) if axis == 0 else node(other, 0, c)
                    end = node(4, other, c) if axis == 0 else node(other, 4, c)
                    first, last = terms.load(start, part), terms.load(end, part)
                    joined = first + jnp.where(has_before, pick(last, before), 0.0)
                    terms.store(start, joined, part)
                    terms.store(end, jnp.where(has_after, pick(joined, after), last), part)
        return carry

    lax.fori_loop(0, vectors // 8, one, 0)


def pack_lower(low, face_out, vectors):
    upper = upper_lanes(vectors)
    for i in range(13):
        second = min(2 * i + 1, 24)
        face_out[i] = jnp.where(upper, up_layer(low[second]), low[2 * i]).astype(BF16)


def pack_upper(top, face_out, vectors):
    upper = upper_lanes(vectors)
    for i in range(13):
        second = min(2 * i + 1, 24)
        face_out[i] = jnp.where(upper, top[2 * i], down_layer(top[second])).astype(BF16)


def from_below(packed, ab):
    return packed if ab % 2 == 1 else down_layer(packed)


def from_above(packed, ab):
    return packed if ab % 2 == 1 else up_layer(packed)


def first_faces_kernel(
    vectors, wave_mid, wave_top, mass_mid, mass_top, ghost, kinetic, coefficient,
    values, wave_low, mass_low, low, top, face_down, face_up,
):
    upper, upper_one = upper_lanes(vectors), upper_lanes(1)
    for ab in range(25):
        packed = ghost[ab // 2]
        wave_low[ab] = jnp.where(upper, up_layer(wave_top[ab]), from_below(packed[0:vectors], ab))
        mass_low[ab : ab + 1, :] = jnp.where(
            upper_one,
            up_layer(mass_top[ab : ab + 1, :]),
            from_below(packed[vectors : vectors + 1], ab),
        )
    wave, mass = Nodes(wave_low, wave_mid, wave_top), Nodes(mass_low, mass_mid, mass_top)
    for j in ALL_ROWS:
        values[j] = (wave.load(j) * mass.line(j)).astype(BF16).astype(F32)
    terms = Nodes(low, None, top)
    apply_cells(values, terms, kinetic, coefficient, LOW_ROWS + TOP_ROWS, vectors)
    join_layer(terms, (0, 4), vectors)
    pack_lower(low, face_down, vectors)
    pack_upper(top, face_up, vectors)


def rest_kernel(vectors, values, kinetic, coefficient, mid):
    terms = Nodes(None, mid, None)
    apply_cells(values, terms, kinetic, coefficient, MID_ROWS, vectors)
    join_layer(terms, (1, 2, 3), vectors)


def second_faces_kernel(
    vectors, low, mid, top, wave_low, wave_mid, wave_top, mass_low, mass_mid, mass_top,
    above, below, kinetic, coefficient, center_ref, halfwidth_ref,
    values, base_mid, base_top, low_out, face_down,
):
    upper = upper_lanes(vectors)
    center = center_ref[0]
    inverse = 1.0 / jnp.full((1, LANES), halfwidth_ref[0], F32)
    again = (-2.0 * center) * inverse
    sums = Nodes(low, mid, top)
    wave, mass = Nodes(wave_low, wave_mid, wave_top), Nodes(mass_low, mass_mid, mass_top)
    base = Nodes(None, base_mid, base_top)

    def degree_one(j, total):
        one = (mass.line(j) * total - center * wave.load(j)) * inverse
        values[j] = (one * mass.line(j)).astype(BF16).astype(F32)
        if j % 5 > 0:
            base.store(j, again * one - wave.load(j))

    for ab in range(25):
        first, last = low[ab], top[ab]
        shared = first + up_layer(last)
        incoming = from_below(below[ab // 2].astype(F32), ab)
        degree_one(5 * ab, jnp.where(upper, shared, first + incoming))
        incoming = from_above(above[ab // 2].astype(F32), ab)
        degree_one(5 * ab + 4, jnp.where(upper, last + incoming, down_layer(shared)))
        for c in range(1, 4):
            degree_one(5 * ab + c, mid[3 * ab + c - 1])
    terms = Nodes(low_out, None, None)
    apply_cells(values, terms, kinetic, coefficient, LOW_ROWS, vectors)
    join_layer(terms, (0,), vectors)
    pack_lower(low_out, face_down, vectors)


def kept_lanes(ab):
    lane = lane_index(1)
    keep = None
    if ab // 5 == 4:
        keep = axis_place(lane, 0) == 7
    if ab % 5 == 4:
        last = axis_place(lane, 1) == 7
        keep = last if keep is None else jnp.logical_and(keep, last)
    return keep


def scatter_rows(vectors, groups, rows, conn, value_of, total):
    start = 0
    while start < len(rows):
        count = 5 if len(rows) - start == 5 else min(4, len(rows) - start)
        width = count * LANES
        pieces, slots = [], []
        for j in rows[start : start + count]:
            keep, slot = kept_lanes(j // 5), conn[j : j + 1, :]
            slots.append(slot if keep is None else jnp.where(keep, slot, 65535))
            pieces.append(value_of(j).astype(BF16))
        value, slot = jnp.concatenate(pieces, 1), jnp.concatenate(slots, 1)
        group = slot >> 8
        wide = jnp.broadcast_to(group.astype(F32).astype(BF16), (vectors, width))
        spread = [jnp.where(wide == BF16(h), value, BF16(0)) for h in range(groups)]
        spare = total.shape[0] - vectors * groups
        group_row = lax.broadcasted_iota(I32, (spare, width), 0)
        held = jnp.where(group_row == jnp.broadcast_to(group, (spare, width)), 1.0, 0.0)
        spread.append(held.astype(BF16))
        moved = lax.dot_general(
            jnp.concatenate(spread, 0),
            one_hot(slot, width),
            (((1,), (1,)), ((), ())),
            preferred_element_type=F32,
        )
        if start == 0:
            total[...] = moved
        else:
            total[...] += moved
        start += count


def second_rest_kernel(
    vectors, values, kinetic, coefficient, low, mass_mid, mass_top, base_mid, base_top, conn,
    wave_hbm, center_ref, halfwidth_ref, total, done_top, alone, mid, top, wave_in, sems,
):
    copy = pltpu.make_async_copy(wave_hbm, wave_in, sems.at[0])
    copy.start()
    groups = wave_in.shape[1] // 256
    center = center_ref[0]
    inverse = 1.0 / jnp.full((1, LANES), halfwidth_ref[0], F32)
    terms = Nodes(None, mid, top)
    apply_cells(values, terms, kinetic, coefficient, MID_ROWS + TOP_ROWS, vectors)
    join_layer(terms, (1, 2, 3, 4), vectors)
    upper = upper_lanes(vectors)
    for ab in range(25):
        last = top[ab]
        joined = jnp.where(upper, last, down_layer(low[ab]) + last)
        line = (2.0 * inverse) * mass_top[ab : ab + 1, :]
        done_top[ab] = base_top[ab] + line * joined

    def value_of(j):
        row = 3 * (j // 5) + j % 5 - 1
        return base_mid[row] + (2.0 * inverse) * mass_mid[row : row + 1, :] * mid[row]

    scatter_rows(vectors, groups, MID_ROWS, conn, value_of, total)
    copy.wait()
    wide_inverse = jnp.concatenate([inverse, inverse], 1)
    for h in range(groups):
        wave = wave_in[:, 256 * h : 256 * (h + 1)]
        one = -center * wave * wide_inverse
        alone[:, 256 * h : 256 * (h + 1)] = (
            (-2.0 * center) * wide_inverse * one - wave
        ).astype(BF16)


def scatter_top_kernel(
    vectors, conn, before, done_top, mass_top, above, alone, halfwidth_ref, out_ref, total
):
    groups = alone.shape[1] // 256
    base = vectors * groups
    upper = upper_lanes(vectors)
    inverse = 1.0 / jnp.full((1, LANES), halfwidth_ref[0], F32)

    def value_of(j):
        ab = j // 5
        incoming = from_above(above[ab // 2].astype(F32), ab)
        share = (2.0 * inverse) * mass_top[ab : ab + 1, :] * incoming
        return done_top[ab] + jnp.where(upper, share, 0.0)

    scatter_rows(vectors, groups, TOP_ROWS, conn, value_of, total)
    quarter = groups // out_ref.shape[0]
    for h in range(groups):
        rows = slice(vectors * h, vectors * (h + 1))
        count = total[base + h : base + h + 1, :] + before[base + h : base + h + 1, :]
        value = total[rows, :] + before[rows, :]
        own = alone[:, 256 * h : 256 * (h + 1)].astype(F32)
        at = h % quarter
        out_ref[h // quarter, :, 256 * at : 256 * (at + 1)] = jnp.where(
            count > 0.5, value, own
        ).astype(BF16)


def stream_rows(earlier_hbm, earlier, sems):
    count = sems.shape[0]
    size = earlier.shape[0] // count
    copies = []
    for i in range(count):
        rows = slice(size * i, size * (i + 1))
        copy = pltpu.make_async_copy(earlier_hbm.at[rows, :], earlier.at[rows, :], sems.at[i])
        copy.start()
        copies.append((rows, copy))
    return copies


def project_kernel(
    cores, parts, share, earlier_hbm, quarter, core_ref, keep, send, earlier, sems
):
    half = share // 2
    for i, (rows, copy) in enumerate(stream_rows(earlier_hbm, earlier, sems)):
        copy.wait()
        product = lax.dot_general(
            earlier[rows, :], quarter[...], (((1,), (1,)), ((), ())), preferred_element_type=F32
        )
        chunk = product.shape[0] // (cores * parts * share)
        lines = chunk * parts * half
        place = slice(lines * i, lines * (i + 1))
        product = product.reshape(chunk, cores, parts, share, product.shape[-1])
        for core in range(cores):
            mine = product[:, core].reshape(chunk * parts, share, product.shape[-1])
            mine = jnp.concatenate([mine[:, :half], mine[:, half:]], 2)
            mine = mine.reshape(lines, mine.shape[-1])

            @pl.when(core_ref[0] == core)
            def _():
                keep[place, :] = mine

            @pl.when(core_ref[0] != core)
            def _():
                send[place, :] = mine


def filter_kernel(
    cores, parts, share, mine, theirs, earlier_hbm, quarter, core_ref, out_ref, low, earlier, sems
):
    copies = stream_rows(earlier_hbm, earlier, sems)
    half = share // 2
    columns = mine.shape[-1] // 2
    block = parts * share

    def unpack(ref, core):
        value = ref[...].astype(F32)
        value = jnp.concatenate([value[:, :, :columns], value[:, :, columns:]], 1)
        value = value.reshape(value.shape[0] // parts, block, columns)
        for i in range(value.shape[0]):
            at = (cores * i + core) * block
            low[at : at + block, :] = value[i].astype(BF16)

    for core in range(cores):

        @pl.when(core_ref[0] == core)
        def _():
            unpack(mine, core)
            unpack(theirs, 1 - core)

    out_ref[...] = quarter[...].astype(F32)
    for rows, copy in copies:
        copy.wait()
        out_ref[...] -= lax.dot_general(
            low[rows, :], earlier[rows, :], (((0,), (0,)), ((), ())), preferred_element_type=F32
        )


VMEM_SPEC = pl.BlockSpec(memory_space=pltpu.VMEM)
SMEM_SPEC = pl.BlockSpec(memory_space=pltpu.SMEM)
HBM_SPEC = pl.BlockSpec(memory_space=pltpu.HBM)


def call(kernel, name, out_shape, specs, scratch, *operands):
    return pl.pallas_call(
        kernel,
        out_shape=out_shape,
        in_specs=[{"v": VMEM_SPEC, "s": SMEM_SPEC, "h": HBM_SPEC}[letter] for letter in specs],
        out_specs=jax.tree.map(lambda _: VMEM_SPEC, out_shape),
        scratch_shapes=scratch,
        compiler_params=pltpu.CompilerParams(vmem_limit_bytes=VMEM_LIMIT),
        name=name,
    )(*[
        pltpu.with_memory_space_constraint(operand, pltpu.HBM) if letter == "h" else operand
        for letter, operand in zip(specs, operands)
    ])


def passed_along(value, axis, steps):
    count = lax.axis_size(axis)
    leading, last = (max(0, -steps), min(count, count - steps))
    return lax.ppermute(value, axis, [(source, source + steps) for source in range(leading, last)])


def per_device(
    wave_block, connectivity, send_list, levels, live_cells, potential, mass_scale,
    center, halfwidth, earlier_vectors,
):
    vectors, owned = wave_block.shape
    groups = owned // 256
    table_rows = vectors * groups + 48
    cells, parts = lax.axis_size("cells"), lax.axis_size("vecs")
    devices, cores = cells * parts, 2
    center, halfwidth = center.reshape(1), halfwidth.reshape(1)

    def shape(*sizes, kind=F32):
        return jax.ShapeDtypeStruct(sizes, kind)

    def rows(count):
        return shape(count, vectors, LANES)

    def lines(count):
        return shape(count, LANES)

    packed = shape(13, vectors, LANES, kind=BF16)
    scratch_rows = lambda count: pltpu.VMEM((count, vectors, LANES), F32)
    wave_scratch = pltpu.VMEM((vectors, owned), F32)

    table, conn, wave_top, mass_top, face = call(
        lambda *refs: gather_face_kernel(vectors, *refs),
        "gather_face",
        (
            shape(table_rows, 512, kind=BF16), shape(125, LANES, kind=I32), rows(25), lines(25),
            shape(13, vectors + 8, LANES),
        ),
        "hhh",
        [wave_scratch, pltpu.VMEM((owned // LANES, LANES), F32), pltpu.SemaphoreType.DMA((3,))],
        connectivity, wave_block, mass_scale.reshape(owned // LANES, LANES),
    )
    ghost = passed_along(face, "cells", 1)
    wave_mid, mass_mid, kinetic, coefficient = call(
        lambda *refs: gather_rest_kernel(vectors, groups, *refs),
        "gather_rest",
        (rows(75), lines(75), lines(8), lines(125)),
        "vvhhs",
        [pltpu.VMEM((1, LANES), I32), pltpu.SemaphoreType.DMA((2,))],
        table, conn, potential, levels.reshape(1, LANES), live_cells,
    )
    values, wave_low, mass_low, low, top, face_down, face_up = call(
        lambda *refs: first_faces_kernel(vectors, *refs),
        "first_faces",
        (rows(125), rows(25), lines(25), rows(25), rows(25), packed, packed),
        "vvvvvvv",
        [],
        wave_mid, wave_top, mass_mid, mass_top, ghost, kinetic, coefficient,
    )
    above = passed_along(face_down, "cells", -1)
    below = passed_along(face_up, "cells", 1)
    mid = call(
        lambda *refs: rest_kernel(vectors, *refs), "first_rest", rows(75), "vvv", [],
        values, kinetic, coefficient,
    )
    values, base_mid, base_top, low, face_down = call(
        lambda *refs: second_faces_kernel(vectors, *refs),
        "second_faces",
        (rows(125), rows(75), rows(25), rows(25), packed),
        "v" * 13 + "ss",
        [],
        low, mid, top, wave_low, wave_mid, wave_top, mass_low, mass_mid, mass_top,
        above, below, kinetic, coefficient, center, halfwidth,
    )
    above = passed_along(face_down, "cells", -1)
    before, done_top, alone = call(
        lambda *refs: second_rest_kernel(vectors, *refs),
        "second_rest",
        (shape(table_rows, 256), rows(25), shape(vectors, owned, kind=BF16)),
        "v" * 9 + "hss",
        [scratch_rows(75), scratch_rows(25), wave_scratch, pltpu.SemaphoreType.DMA((1,))],
        values, kinetic, coefficient, low, mass_mid, mass_top, base_mid, base_top, conn,
        wave_block, center, halfwidth,
    )
    rounded = call(
        lambda *refs: scatter_top_kernel(vectors, *refs),
        "scatter_top",
        shape(parts, vectors, owned // parts, kind=BF16),
        "vvvvvvs",
        [pltpu.VMEM((table_rows, 256), F32)],
        conn, before, done_top, mass_top, above, alone, halfwidth,
    )
    quarter = lax.all_to_all(rounded, "vecs", split_axis=0, concat_axis=0, tiled=True)
    quarter = quarter.reshape(parts * vectors, owned // parts)
    total_vectors = parts * vectors
    share = earlier_vectors.shape[0] // devices
    half, peers = share // 2, devices // cores
    core = (lax.axis_index("cells") % cores).astype(I32).reshape(1)
    pair = [(i, i ^ 1) for i in range(cells)]
    same_core = [
        [(cores * block + k) * parts + part for block in range(cells // cores) for part in range(parts)]
        for k in range(cores)
    ]
    sent = shape(peers * half, 2 * total_vectors)
    blocks = math.gcd(8, peers // parts)
    earlier_scratch = [
        pltpu.VMEM(earlier_vectors.shape, BF16), pltpu.SemaphoreType.DMA((blocks,))
    ]
    keep, send = call(
        lambda *refs: project_kernel(cores, parts, share, *refs),
        "project", (sent, sent), "hvs", earlier_scratch, earlier_vectors, quarter, core,
    )
    shares = (keep + lax.ppermute(send, "cells", pair)).reshape(peers, half, 2 * total_vectors)
    shares = lax.all_to_all(
        shares, AXES, split_axis=0, concat_axis=0, tiled=True, axis_index_groups=same_core
    )
    own = jnp.sum(shares, 0)
    own_rows = own.reshape(half, 2, total_vectors).transpose(1, 0, 2).reshape(share, total_vectors)
    mine = jnp.broadcast_to(own.astype(BF16)[None], (peers, half, 2 * total_vectors))
    mine = lax.all_to_all(
        mine, AXES, split_axis=0, concat_axis=0, tiled=True, axis_index_groups=same_core
    )
    theirs = lax.ppermute(mine, "cells", pair)
    filtered = call(
        lambda *refs: filter_kernel(cores, parts, share, *refs),
        "filter",
        shape(total_vectors, owned // parts),
        "vvhvs",
        [pltpu.VMEM((devices * share, total_vectors), BF16)] + earlier_scratch,
        mine, theirs, earlier_vectors, quarter, core,
    )
    return (filtered, own_rows)


def solution(mesh):
    in_specs = (
        P("vecs", "cells"),
        P(None, "cells"),
        P("cells"),
        P("cells"),
        P("cells"),
        P(None, "cells"),
        P("cells"),
        P(),
        P(),
        P(None, AXES),
    )
    out_specs = (P(None, AXES), P(AXES, None))
    return jax.shard_map(
        per_device, mesh=mesh, in_specs=in_specs, out_specs=out_specs, check_vma=False
    )
```

```python
import math

import jax
import jax.numpy as jnp
import numpy as np
from jax import lax
from jax.experimental import pallas as pl
from jax.experimental.pallas import tpu as pltpu
from jax.sharding import PartitionSpec as P

F32, BF16, I32 = jnp.float32, jnp.bfloat16, jnp.int32
AXES = ("cells", "vecs")
LANES = 128
BLOCKS = 8
VMEM_LIMIT = 20 * 2**20


def gll_tables():
    root_value = math.sqrt(3.0 / 7.0)
    points = np.array([-1.0, -root_value, 0.0, root_value, 1.0])
    weights = np.array([0.1, 49.0 / 90.0, 32.0 / 45.0, 49.0 / 90.0, 0.1])
    barycentric = np.ones(5)
    for node_index in range(5):
        for other_node in range(5):
            if other_node != node_index:
                barycentric[node_index] = barycentric[node_index] / (
                    points[node_index] - points[other_node]
                )
    derivative = np.zeros((5, 5))
    for row_index in range(5):
        for col_index in range(5):
            if row_index != col_index:
                derivative[row_index, col_index] = (
                    barycentric[col_index]
                    / barycentric[row_index]
                    / (points[row_index] - points[col_index])
                )
        derivative[row_index, row_index] = -np.sum(derivative[row_index])
    mass_one = np.zeros((5, 5))
    for node_index in range(5):
        mass_one[node_index, node_index] = weights[node_index]
    laplace_one = derivative.T @ mass_one @ derivative
    stiffness = (
        np.kron(np.kron(laplace_one, mass_one), mass_one)
        + np.kron(np.kron(mass_one, laplace_one), mass_one)
        + np.kron(np.kron(mass_one, mass_one), laplace_one)
    )
    quadrature = np.kron(np.kron(weights, weights), weights)
    return (stiffness.astype(np.float32), quadrature.astype(np.float32))


STIFFNESS, QUADRATURE = gll_tables()
STIFFNESS = STIFFNESS.astype(jnp.bfloat16).astype(np.float32)


def node(a, b, c):
    return 25 * a + 5 * b + c


def lane_index(rows):
    return lax.broadcasted_iota(I32, (rows, LANES), 1)


def axis_bits(lane, axis):
    return [(lane >> bit) & 1 for bit in ((0, 3, 5), (1, 4, 6))[axis]]


def axis_place(lane, axis):
    low, mid, high = axis_bits(lane, axis)
    return low + 2 * mid + 4 * high


def below_of(lane, axis):
    low, mid, high = axis_bits(lane, axis)
    scale = 1 + axis
    step = jnp.where(low == 1, 1, jnp.where(mid == 1, 7, 23)) * scale
    first = axis_place(lane, axis) == 0
    return jnp.where(first, lane, lane - step), jnp.logical_not(first)


def above_of(lane, axis):
    low, mid, high = axis_bits(lane, axis)
    scale = 1 + axis
    step = jnp.where(low == 0, 1, jnp.where(mid == 0, 7, 23)) * scale
    last = axis_place(lane, axis) == 7
    return jnp.where(last, lane, lane + step), jnp.logical_not(last)


def pick(values, index):
    return jnp.take_along_axis(values, index, axis=1)


def up_layer(values):
    return pltpu.roll(values, 4, 1)


def down_layer(values):
    return pltpu.roll(values, LANES - 4, 1)


def split_low(values):
    high = values.astype(BF16)
    return high, (values - high.astype(F32)).astype(BF16)


class Nodes:
    def __init__(self, low, mid, top):
        self.low, self.mid, self.top = low, mid, top

    def at(self, j):
        ab, c = divmod(j, 5)
        if c == 0:
            return self.low, ab
        if c == 4:
            return self.top, ab
        return self.mid, 3 * ab + c - 1

    def load(self, j, part=slice(None)):
        ref, row = self.at(j)
        return ref[row, part, :]

    def store(self, j, value, part=slice(None)):
        ref, row = self.at(j)
        ref[row, part, :] = value

    def line(self, j):
        ref, row = self.at(j)
        return ref[row : row + 1, :]

    def store_line(self, j, value):
        ref, row = self.at(j)
        ref[row : row + 1, :] = value


ALL_ROWS = list(range(125))
MID_ROWS = [j for j in ALL_ROWS if j % 5 in (1, 2, 3)]
LOW_ROWS = [j for j in ALL_ROWS if j % 5 == 0]
TOP_ROWS = [j for j in ALL_ROWS if j % 5 == 4]


def upper_lanes(rows):
    return (lane_index(rows) >> 2) & 1 == 1


def one_hot(slots, width):
    place = lax.broadcasted_iota(I32, (256, width), 0).astype(F32).astype(BF16)
    within = jnp.broadcast_to((slots & 255).astype(F32).astype(BF16), (256, width))
    return jnp.where(place == within, BF16(1), BF16(0))


AXIS_MASK = (1 + 8 + 32, 2 + 16 + 64)


def place_bits(place, axis):
    return [(place & 1) + (place & 2) * 4 + (place & 4) * 8, (place & 1) * 2 + (place & 2) * 8 + (place & 4) * 16][axis]


def tile_plan(layers):
    tiles = [("all", [node(a, b, c)]) for a in range(4) for b in range(4) for c in layers]
    for axis in range(2):
        rows = [
            node(4, k, c) if axis == 0 else node(k, 4, c)
            for k in range(5 - axis)
            for c in layers
        ]
        tiles += [(axis, rows[i : i + 8]) for i in range(0, len(rows), 8)]
    return tiles


MID_PLAN, TOP_PLAN = tile_plan((1, 2, 3)), tile_plan((4,))


def tile_groups(plan):
    count = len(plan)
    fives = count % 4
    sizes = [5] * fives + [4] * ((count - 5 * fives) // 4)
    starts = np.cumsum([0] + sizes)
    return [(int(start), size) for start, size in zip(starts, sizes)]


def pack_tile(kind, rows, load, empty):
    if kind == "all":
        return load(rows[0])
    lane = lane_index(8)
    place, last = axis_place(lane, kind), lane | AXIS_MASK[kind]
    tile = jnp.full((8, LANES), empty)
    for i, j in enumerate(rows):
        tile = jnp.where(place == i, pick(load(j), last), tile)
    return tile


def repeated_places(kind, rows):
    return [i for i, j in enumerate(rows) if kind == 0 and j // 5 == 24]


def pack_slots(plan, conn, slots):
    def load(j):
        return jnp.broadcast_to(conn[j : j + 1, :], (8, LANES))

    for i, (kind, rows) in enumerate(plan):
        tile = pack_tile(kind, rows, load, jnp.int32(65535))
        slots[i : i + 1, :] = tile[0:1, :]


def unpack_tiles(plan, extra, load, store):
    lane = lane_index(8)
    for axis in (1, 0):
        after, has_after = above_of(lane, axis)
        for i, (kind, rows) in enumerate(plan):
            if kind != axis:
                continue
            tile = extra(i)
            for place, j in enumerate(rows):
                source = (lane & ~AXIS_MASK[axis]) | place_bits(place, axis)
                inner = pick(load(j - (100 if axis == 0 else 20)), after)
                store(j, jnp.where(has_after, inner, pick(tile, source)))


def gather_rows(vectors, groups, plan, row_of, slots_ref, table, wave, mass, wave_extra, mass_extra):
    base = vectors * groups
    whole = sum(kind == "all" for kind, _ in plan)
    for start, count in tile_groups(plan):
        width = count * LANES
        slots = jnp.concatenate([slots_ref[start + i : start + i + 1, :] for i in range(count)], 1)
        chosen = one_hot(slots, width)
        found = jnp.dot(
            table[...], jnp.concatenate([chosen, chosen], 0), preferred_element_type=F32
        )
        group = slots >> 8
        wide = jnp.broadcast_to(group, (vectors, width))
        total = jnp.zeros((vectors, width), F32)
        for h in range(groups):
            total = jnp.where(wide == h, found[vectors * h : vectors * (h + 1)], total)
        group_row = lax.broadcasted_iota(I32, (groups, width), 0)
        mine = group_row == jnp.broadcast_to(group, (groups, width))
        line = jnp.sum(jnp.where(mine, found[base : base + groups], 0.0), 0, keepdims=True)
        for i in range(count):
            kind, rows = plan[start + i]
            columns = slice(LANES * i, LANES * (i + 1))
            if kind == "all":
                row = row_of(rows[0])
                wave[row] = total[:, columns]
                mass[row : row + 1, :] = line[:, columns]
            else:
                wave_extra[start + i - whole] = total[:, columns]
                mass_extra[start + i - whole] = jnp.broadcast_to(line[:, columns], (8, LANES))
    for half in range(vectors // 8):
        part = slice(8 * half, 8 * (half + 1))

        def store(j, value):
            wave[row_of(j), part, :] = value

        unpack_tiles(
            plan, lambda i: wave_extra[i - whole, part, :], lambda j: wave[row_of(j), part, :], store
        )

    def store_line(j, value):
        mass[row_of(j) : row_of(j) + 1, :] = value[0:1, :]

    def load_line(j):
        return jnp.broadcast_to(mass[row_of(j) : row_of(j) + 1, :], (8, LANES))

    unpack_tiles(plan, lambda i: mass_extra[i - whole], load_line, store_line)


def mid_row(j):
    return 3 * (j // 5) + j % 5 - 1


def top_row(j):
    return j // 5


def gather_face_kernel(
    vectors, conn_hbm, wave_hbm, mass_hbm, table, conn, slots, wave_top, mass_top, face_out,
    wave_in, mass_in, wave_extra, mass_extra, sems,
):
    copies = [
        pltpu.make_async_copy(wave_hbm, wave_in, sems.at[0]),
        pltpu.make_async_copy(mass_hbm, mass_in, sems.at[1]),
        pltpu.make_async_copy(conn_hbm, conn, sems.at[2]),
    ]
    for copy in copies:
        copy.start()
    for copy in copies:
        copy.wait()
    groups = wave_in.shape[1] // 256
    base = vectors * groups
    high, low = split_low(wave_in[...])
    for h in range(groups):
        table[vectors * h : vectors * (h + 1), 0:256] = high[:, 256 * h : 256 * (h + 1)]
        table[vectors * h : vectors * (h + 1), 256:512] = low[:, 256 * h : 256 * (h + 1)]
    for half in range(2):
        high, low = split_low(mass_in[pl.ds(half, groups, stride=2), :])
        spare = jnp.zeros((table.shape[0] - base - groups, LANES), F32)
        columns = slice(LANES * half, LANES * (half + 1))
        table[base:, columns] = jnp.concatenate([high.astype(F32), spare], 0).astype(BF16)
        columns = slice(256 + LANES * half, 256 + LANES * (half + 1))
        table[base:, columns] = jnp.concatenate([low.astype(F32), spare], 0).astype(BF16)
    pack_slots(TOP_PLAN, conn, slots)
    gather_rows(
        vectors, groups, TOP_PLAN, top_row, slots, table, wave_top, mass_top, wave_extra, mass_extra
    )
    upper, upper_one = upper_lanes(vectors), upper_lanes(1)
    for i in range(13):
        second = min(2 * i + 1, 24)
        face_out[i, 0:vectors, :] = jnp.where(upper, wave_top[2 * i], down_layer(wave_top[second]))
        packed = jnp.where(
            upper_one,
            mass_top[2 * i : 2 * i + 1, :],
            down_layer(mass_top[second : second + 1, :]),
        )
        face_out[i, vectors : vectors + 8, :] = jnp.broadcast_to(packed, (8, LANES))


def gather_rest_kernel(
    vectors, groups, table, conn, potential_hbm, levels_hbm, live_ref,
    slots, wave_mid, mass_mid, kinetic, coefficient, levels_in, wave_extra, mass_extra, sems,
):
    copies = [
        pltpu.make_async_copy(potential_hbm, coefficient, sems.at[0]),
        pltpu.make_async_copy(levels_hbm, levels_in, sems.at[1]),
    ]
    for copy in copies:
        copy.start()
    pack_slots(MID_PLAN, conn, slots)
    gather_rows(
        vectors, groups, MID_PLAN, mid_row, slots, table, wave_mid, mass_mid, wave_extra, mass_extra
    )
    copies[0].wait()
    copies[1].wait()
    size = jnp.exp2(-levels_in[...].astype(F32))
    in_use = jnp.where(lane_index(1) < live_ref[0], 1.0, 0.0).astype(F32)
    kinetic[...] = jnp.broadcast_to(size / 4.0 * in_use, (8, LANES))
    volume = size * size * size / 8.0 * in_use
    for j in ALL_ROWS:
        line = volume * float(QUADRATURE[j]) * coefficient[j : j + 1, :]
        coefficient[j : j + 1, :] = line


def apply_cells(values, terms, kinetic, coefficient, rows, vectors):
    def one(t, carry):
        part = pl.ds(pl.multiple_of(8 * t, 8), 8)
        for j in rows:
            total = None
            for k in np.flatnonzero(STIFFNESS[j]):
                term = values[int(k), part, :] * float(STIFFNESS[j, k])
                total = term if total is None else total + term
            weight = jnp.broadcast_to(coefficient[j : j + 1, :], (8, LANES))
            terms.store(j, kinetic[...] * total + weight * values[j, part, :], part)
        return carry

    lax.fori_loop(0, vectors // 8, one, 0)


def join_layer(terms, layers, vectors):
    lane = lane_index(8)
    moves = [below_of(lane, axis) + above_of(lane, axis) for axis in range(2)]

    def one(t, carry):
        part = pl.ds(pl.multiple_of(8 * t, 8), 8)
        for axis in range(2):
            before, has_before, after, has_after = moves[axis]
            for other in range(5):
                for c in layers:
                    start = node(0, other, c) if axis == 0 else node(other, 0, c)
                    end = node(4, other, c) if axis == 0 else node(other, 4, c)
                    first, last = terms.load(start, part), terms.load(end, part)
                    joined = first + jnp.where(has_before, pick(last, before), 0.0)
                    terms.store(start, joined, part)
                    terms.store(end, jnp.where(has_after, pick(joined, after), last), part)
        return carry

    lax.fori_loop(0, vectors // 8, one, 0)


def pack_lower(low, face_out, vectors):
    upper = upper_lanes(vectors)
    for i in range(13):
        second = min(2 * i + 1, 24)
        face_out[i] = jnp.where(upper, up_layer(low[second]), low[2 * i]).astype(BF16)


def pack_upper(top, face_out, vectors):
    upper = upper_lanes(vectors)
    for i in range(13):
        second = min(2 * i + 1, 24)
        face_out[i] = jnp.where(upper, top[2 * i], down_layer(top[second])).astype(BF16)


def from_below(packed, ab):
    return packed if ab % 2 == 1 else down_layer(packed)


def from_above(packed, ab):
    return packed if ab % 2 == 1 else up_layer(packed)


def first_faces_kernel(
    vectors, wave_mid, wave_top, mass_mid, mass_top, ghost, kinetic, coefficient,
    values, wave_low, mass_low, low, top, face_down, face_up,
):
    upper, upper_one = upper_lanes(vectors), upper_lanes(1)
    for ab in range(25):
        packed = ghost[ab // 2]
        wave_low[ab] = jnp.where(upper, up_layer(wave_top[ab]), from_below(packed[0:vectors], ab))
        mass_low[ab : ab + 1, :] = jnp.where(
            upper_one,
            up_layer(mass_top[ab : ab + 1, :]),
            from_below(packed[vectors : vectors + 1], ab),
        )
    wave, mass = Nodes(wave_low, wave_mid, wave_top), Nodes(mass_low, mass_mid, mass_top)
    for j in ALL_ROWS:
        values[j] = (wave.load(j) * mass.line(j)).astype(BF16).astype(F32)
    terms = Nodes(low, None, top)
    apply_cells(values, terms, kinetic, coefficient, LOW_ROWS + TOP_ROWS, vectors)
    join_layer(terms, (0, 4), vectors)
    pack_lower(low, face_down, vectors)
    pack_upper(top, face_up, vectors)


def rest_kernel(vectors, values, kinetic, coefficient, mid):
    terms = Nodes(None, mid, None)
    apply_cells(values, terms, kinetic, coefficient, MID_ROWS, vectors)
    join_layer(terms, (1, 2, 3), vectors)


def second_faces_kernel(
    vectors, low, mid, top, wave_low, wave_mid, wave_top, mass_low, mass_mid, mass_top,
    above, below, kinetic, coefficient, center_ref, halfwidth_ref,
    values, base_mid, base_top, low_out, face_down,
):
    upper = upper_lanes(vectors)
    center = center_ref[0]
    inverse = 1.0 / jnp.full((1, LANES), halfwidth_ref[0], F32)
    again = (-2.0 * center) * inverse
    sums = Nodes(low, mid, top)
    wave, mass = Nodes(wave_low, wave_mid, wave_top), Nodes(mass_low, mass_mid, mass_top)
    base = Nodes(None, base_mid, base_top)

    def degree_one(j, total):
        one = (mass.line(j) * total - center * wave.load(j)) * inverse
        values[j] = (one * mass.line(j)).astype(BF16).astype(F32)
        if j % 5 > 0:
            base.store(j, again * one - wave.load(j))

    for ab in range(25):
        first, last = low[ab], top[ab]
        shared = first + up_layer(last)
        incoming = from_below(below[ab // 2].astype(F32), ab)
        degree_one(5 * ab, jnp.where(upper, shared, first + incoming))
        incoming = from_above(above[ab // 2].astype(F32), ab)
        degree_one(5 * ab + 4, jnp.where(upper, last + incoming, down_layer(shared)))
        for c in range(1, 4):
            degree_one(5 * ab + c, mid[3 * ab + c - 1])
    terms = Nodes(low_out, None, None)
    apply_cells(values, terms, kinetic, coefficient, LOW_ROWS, vectors)
    join_layer(terms, (0,), vectors)
    pack_lower(low_out, face_down, vectors)


def scatter_rows(vectors, groups, plan, slots_ref, load, total):
    for start, count in tile_groups(plan):
        width = count * LANES
        pieces = []
        for kind, rows in plan[start : start + count]:
            halves = []
            for half in range(vectors // 8):
                part = slice(8 * half, 8 * (half + 1))
                halves.append(pack_tile(kind, rows, lambda j: load(j, part), jnp.float32(0)))
            pieces.append(jnp.concatenate(halves, 0).astype(BF16))
        value = jnp.concatenate(pieces, 1)
        slots = []
        for i in range(count):
            slot = slots_ref[start + i : start + i + 1, :]
            for place in repeated_places(*plan[start + i]):
                lane = lane_index(1)
                again = jnp.logical_and(axis_place(lane, 0) == place, axis_place(lane, 1) < 7)
                slot = jnp.where(again, 65535, slot)
            slots.append(slot)
        slot = jnp.concatenate(slots, 1)
        group = slot >> 8
        wide = jnp.broadcast_to(group.astype(F32).astype(BF16), (vectors, width))
        spread = [jnp.where(wide == BF16(h), value, BF16(0)) for h in range(groups)]
        spare = total.shape[0] - vectors * groups
        group_row = lax.broadcasted_iota(I32, (spare, width), 0)
        held = jnp.where(group_row == jnp.broadcast_to(group, (spare, width)), 1.0, 0.0)
        spread.append(held.astype(BF16))
        moved = lax.dot_general(
            jnp.concatenate(spread, 0),
            one_hot(slot, width),
            (((1,), (1,)), ((), ())),
            preferred_element_type=F32,
        )
        if start == 0:
            total[...] = moved
        else:
            total[...] += moved


def second_rest_kernel(
    vectors, values, kinetic, coefficient, low, mass_mid, mass_top, base_mid, base_top, slots,
    wave_hbm, earlier_hbm, center_ref, halfwidth_ref,
    total, done_top, alone, *rest,
):
    earlier, (mid, top, wave_in, sems) = rest[:-4], rest[-4:]
    copy = pltpu.make_async_copy(wave_hbm, wave_in, sems.at[0])
    copy.start()
    loads = []
    for i, part in enumerate(earlier):
        size = part.shape[0]
        source = earlier_hbm.at[size * i : size * (i + 1), :]
        loads.append(pltpu.make_async_copy(source, part, sems.at[1 + i]))
        loads[-1].start()
    groups = wave_in.shape[1] // 256
    center = center_ref[0]
    inverse = 1.0 / jnp.full((1, LANES), halfwidth_ref[0], F32)
    terms = Nodes(None, mid, top)
    apply_cells(values, terms, kinetic, coefficient, MID_ROWS + TOP_ROWS, vectors)
    join_layer(terms, (1, 2, 3, 4), vectors)
    upper = upper_lanes(vectors)
    for ab in range(25):
        last = top[ab]
        joined = jnp.where(upper, last, down_layer(low[ab]) + last)
        line = (2.0 * inverse) * mass_top[ab : ab + 1, :]
        done_top[ab] = base_top[ab] + line * joined

    def load(j, part):
        row = mid_row(j)
        line = (2.0 * inverse) * mass_mid[row : row + 1, :]
        return base_mid[row, part, :] + line * mid[row, part, :]

    scatter_rows(vectors, groups, MID_PLAN, slots, load, total)
    copy.wait()
    wide_inverse = jnp.concatenate([inverse, inverse], 1)
    for h in range(groups):
        wave = wave_in[:, 256 * h : 256 * (h + 1)]
        one = -center * wave * wide_inverse
        alone[:, 256 * h : 256 * (h + 1)] = (
            (-2.0 * center) * wide_inverse * one - wave
        ).astype(BF16)
    for load in loads:
        load.wait()


def scatter_top_kernel(
    vectors, slots, before, done_top, mass_top, above, alone, halfwidth_ref, *rest
):
    outs, (placed, total) = rest[:-2], rest[-2:]
    groups = alone.shape[1] // 256
    base = vectors * groups
    upper = upper_lanes(8)
    inverse = 1.0 / jnp.full((1, LANES), halfwidth_ref[0], F32)

    def load(j, part):
        ab = j // 5
        incoming = from_above(above[ab // 2].astype(F32)[part], ab)
        share = (2.0 * inverse) * mass_top[ab : ab + 1, :] * incoming
        return done_top[ab, part, :] + jnp.where(upper, share, 0.0)

    scatter_rows(vectors, groups, TOP_PLAN, slots, load, total)
    parts, part = len(outs), lax.axis_index("vecs")
    quarter = groups // parts
    for h in range(groups):
        rows = slice(vectors * h, vectors * (h + 1))
        count = total[base + h : base + h + 1, :] + before[base + h : base + h + 1, :]
        value = total[rows, :] + before[rows, :]
        own = alone[:, 256 * h : 256 * (h + 1)].astype(F32)
        at = h % quarter
        away = lax.rem(h // quarter + parts - part, parts)
        placed[away, :, 256 * at : 256 * (at + 1)] = jnp.where(count > 0.5, value, own).astype(BF16)
    for away, out in enumerate(outs):
        out[...] = placed[away]


def project_kernel(cores, parts, share, *rest):
    pieces, earlier, (keep, send, quarter, product) = rest[:parts], rest[parts:-4], rest[-4:]
    for away, piece in enumerate(pieces):
        size = piece.shape[0]
        source = lax.rem(lax.axis_index("vecs") + parts - away, parts)
        quarter[pl.ds(pl.multiple_of(size * source, size), size), :] = piece[...]
    half = share // 2
    columns = quarter.shape[0]
    this_core = lax.rem(lax.axis_index("cells"), cores)
    product[...] = lax.dot_general(
        jnp.concatenate([part[...] for part in earlier], 0),
        quarter[...],
        (((1,), (1,)), ((), ())),
        preferred_element_type=F32,
    )
    block = parts * share

    def pack(core, out):
        for i in range(product.shape[0] // (cores * block)):
            at = (cores * i + core) * block
            mine = product[at : at + block, :].reshape(parts, share, columns)
            out[parts * i : parts * (i + 1)] = jnp.concatenate([mine[:, :half], mine[:, half:]], 2)

    for core in range(cores):

        @pl.when(this_core == core)
        def _():
            pack(core, keep)
            pack(1 - core, send)


def pair_sum_kernel(parts, keep, received, *rest):
    outs, placed = rest[:-1], rest[-1]
    here = lax.axis_index("vecs")
    total = keep[...] + received[...]
    total = total.reshape(total.shape[0] // parts, parts, *total.shape[1:])
    for part in range(parts):
        placed[lax.rem(part + parts - here, parts)] = total[:, part]
    for away, out in enumerate(outs):
        out[...] = placed[away]


def part_sum_kernel(*refs):
    total = refs[0][...]
    for ref in refs[1:-1]:
        total = total + ref[...]
    refs[-1][...] = total


def own_rows_kernel(shares, own_rows, spread):
    own = jnp.sum(shares[...], 0)
    columns = own.shape[1] // 2
    own_rows[...] = jnp.concatenate([own[:, :columns], own[:, columns:]], 0)
    spread[...] = jnp.broadcast_to(own[None], spread.shape).astype(BF16)


def filter_kernel(cores, parts, share, mine, theirs, quarter, *rest):
    earlier, (out_ref, low) = rest[:-2], rest[-2:]
    half = share // 2
    columns = mine.shape[-1] // 2
    block = parts * share

    def unpack(ref, core):
        value = ref[...].astype(F32)
        value = jnp.concatenate([value[:, :, :columns], value[:, :, columns:]], 1)
        value = value.reshape(value.shape[0] // parts, block, columns)
        for i in range(value.shape[0]):
            at = (cores * i + core) * block
            low[at : at + block, :] = value[i].astype(BF16)

    for core in range(cores):

        @pl.when(lax.rem(lax.axis_index("cells"), cores) == core)
        def _():
            unpack(mine, core)
            unpack(theirs, 1 - core)

    width = 256
    for i in range(out_ref.shape[1] // width):
        at = slice(width * i, width * (i + 1))
        product = lax.dot_general(
            low[...],
            jnp.concatenate([part[:, at] for part in earlier], 0),
            (((0,), (0,)), ((), ())),
            preferred_element_type=F32,
        )
        out_ref[:, at] = quarter[:, at].astype(F32) - product


VMEM_SPEC = pl.BlockSpec(memory_space=pltpu.VMEM)
SMEM_SPEC = pl.BlockSpec(memory_space=pltpu.SMEM)
HBM_SPEC = pl.BlockSpec(memory_space=pltpu.HBM)


def call(kernel, name, out_shape, specs, scratch, *operands):
    return pl.pallas_call(
        kernel,
        out_shape=out_shape,
        in_specs=[{"v": VMEM_SPEC, "s": SMEM_SPEC, "h": HBM_SPEC}[letter] for letter in specs],
        out_specs=jax.tree.map(lambda _: VMEM_SPEC, out_shape),
        scratch_shapes=scratch,
        compiler_params=pltpu.CompilerParams(vmem_limit_bytes=VMEM_LIMIT),
        name=name,
    )(*[
        pltpu.with_memory_space_constraint(operand, pltpu.HBM) if letter == "h" else operand
        for letter, operand in zip(specs, operands)
    ])


def passed_along(value, axis, steps):
    count = lax.axis_size(axis)
    leading, last = (max(0, -steps), min(count, count - steps))
    return lax.ppermute(value, axis, [(source, source + steps) for source in range(leading, last)])


def per_device(
    wave_block, connectivity, send_list, levels, live_cells, potential, mass_scale,
    center, halfwidth, earlier_vectors,
):
    vectors, owned = wave_block.shape
    groups = owned // 256
    table_rows = vectors * groups + 48
    cells, parts = lax.axis_size("cells"), lax.axis_size("vecs")
    devices, cores = cells * parts, 2
    turn = lambda away: [(i, (i + away) % parts) for i in range(parts)]
    center, halfwidth = center.reshape(1), halfwidth.reshape(1)

    def shape(*sizes, kind=F32):
        return jax.ShapeDtypeStruct(sizes, kind)

    def rows(count):
        return shape(count, vectors, LANES)

    def lines(count):
        return shape(count, LANES)

    packed = shape(13, vectors, LANES, kind=BF16)
    scratch_rows = lambda count: pltpu.VMEM((count, vectors, LANES), F32)
    wave_scratch = pltpu.VMEM((vectors, owned), F32)

    extra = lambda count: [scratch_rows(count), pltpu.VMEM((count, 8, LANES), F32)]
    table, conn, slots_top, wave_top, mass_top, face = call(
        lambda *refs: gather_face_kernel(vectors, *refs),
        "gather_face",
        (
            shape(table_rows, 512, kind=BF16), shape(125, LANES, kind=I32),
            shape(len(TOP_PLAN), LANES, kind=I32), rows(25), lines(25),
            shape(13, vectors + 8, LANES),
        ),
        "hhh",
        [wave_scratch, pltpu.VMEM((owned // LANES, LANES), F32), *extra(2), pltpu.SemaphoreType.DMA((3,))],
        connectivity, wave_block, mass_scale.reshape(owned // LANES, LANES),
    )
    ghost = passed_along(face, "cells", 1)
    slots_mid, wave_mid, mass_mid, kinetic, coefficient = call(
        lambda *refs: gather_rest_kernel(vectors, groups, *refs),
        "gather_rest",
        (
            shape(len(MID_PLAN), LANES, kind=I32), rows(75), lines(75), lines(8), lines(125),
        ),
        "vvhhs",
        [pltpu.VMEM((1, LANES), I32), *extra(4), pltpu.SemaphoreType.DMA((2,))],
        table, conn, potential, levels.reshape(1, LANES), live_cells,
    )
    values, wave_low, mass_low, low, top, face_down, face_up = call(
        lambda *refs: first_faces_kernel(vectors, *refs),
        "first_faces",
        (rows(125), rows(25), lines(25), rows(25), rows(25), packed, packed),
        "vvvvvvv",
        [],
        wave_mid, wave_top, mass_mid, mass_top, ghost, kinetic, coefficient,
    )
    above = passed_along(face_down, "cells", -1)
    below = passed_along(face_up, "cells", 1)
    mid = call(
        lambda *refs: rest_kernel(vectors, *refs), "first_rest", rows(75), "vvv", [],
        values, kinetic, coefficient,
    )
    values, base_mid, base_top, low, face_down = call(
        lambda *refs: second_faces_kernel(vectors, *refs),
        "second_faces",
        (rows(125), rows(75), rows(25), rows(25), packed),
        "v" * 13 + "ss",
        [],
        low, mid, top, wave_low, wave_mid, wave_top, mass_low, mass_mid, mass_top,
        above, below, kinetic, coefficient, center, halfwidth,
    )
    above = passed_along(face_down, "cells", -1)
    before, done_top, alone, *earlier = call(
        lambda *refs: second_rest_kernel(vectors, *refs),
        "second_rest",
        (
            shape(table_rows, 256), rows(25), shape(vectors, owned, kind=BF16),
            *[shape(earlier_vectors.shape[0] // BLOCKS, owned // parts, kind=BF16)] * BLOCKS,
        ),
        "v" * 9 + "hhss",
        [scratch_rows(75), scratch_rows(25), wave_scratch, pltpu.SemaphoreType.DMA((1 + BLOCKS,))],
        values, kinetic, coefficient, low, mass_mid, mass_top, base_mid, base_top, slots_mid,
        wave_block, earlier_vectors, center, halfwidth,
    )
    pieces = call(
        lambda *refs: scatter_top_kernel(vectors, *refs),
        "scatter_top",
        (shape(vectors, owned // parts, kind=BF16),) * parts,
        "vvvvvvs",
        [pltpu.VMEM((parts, vectors, owned // parts), BF16), pltpu.VMEM((table_rows, 256), F32)],
        slots_top, before, done_top, mass_top, above, alone, halfwidth,
    )
    pieces = [
        lax.ppermute(piece, "vecs", turn(away)) if away else piece
        for away, piece in enumerate(pieces)
    ]
    total_vectors = parts * vectors
    share = earlier_vectors.shape[0] // devices
    half, peers = share // 2, devices // cores
    pair = [(i, i ^ 1) for i in range(cells)]
    same_core = [
        [(cores * block + k) * parts + part for block in range(cells // cores) for part in range(parts)]
        for k in range(cores)
    ]
    sent = shape(peers, half, 2 * total_vectors)
    keep, send, quarter = call(
        lambda *refs: project_kernel(cores, parts, share, *refs),
        "project",
        (sent, sent, shape(total_vectors, owned // parts, kind=BF16)),
        "v" * (parts + BLOCKS),
        [pltpu.VMEM((earlier_vectors.shape[0], total_vectors), F32)],
        *pieces, *earlier,
    )
    blocks = cells // cores
    share_shape = shape(blocks, half, 2 * total_vectors)
    pieces = call(
        lambda *refs: pair_sum_kernel(parts, *refs),
        "pair_sum", (share_shape,) * parts, "vv",
        [pltpu.VMEM((parts,) + share_shape.shape, F32)],
        keep, lax.ppermute(send, "cells", pair),
    )
    pieces = [
        lax.ppermute(piece, "vecs", turn(away)) if away else piece
        for away, piece in enumerate(pieces)
    ]
    shares = call(part_sum_kernel, "part_sum", share_shape, "v" * parts, [], *pieces)
    shares = lax.all_to_all(
        shares, "cells", split_axis=0, concat_axis=0, tiled=True,
        axis_index_groups=[[cores * block + k for block in range(blocks)] for k in range(cores)],
    )
    own_rows, mine = call(
        own_rows_kernel,
        "own_rows",
        (shape(share, total_vectors), shape(peers, half, 2 * total_vectors, kind=BF16)),
        "v", [], shares,
    )
    mine = lax.all_to_all(
        mine, AXES, split_axis=0, concat_axis=0, tiled=True, axis_index_groups=same_core
    )
    theirs = lax.ppermute(mine, "cells", pair)
    filtered = call(
        lambda *refs: filter_kernel(cores, parts, share, *refs),
        "filter",
        shape(total_vectors, owned // parts),
        "vvv" + "v" * BLOCKS,
        [pltpu.VMEM((devices * share, total_vectors), BF16)],
        mine, theirs, quarter, *earlier,
    )
    return (filtered, own_rows)


def solution(mesh):
    in_specs = (
        P("vecs", "cells"),
        P(None, "cells"),
        P("cells"),
        P("cells"),
        P("cells"),
        P(None, "cells"),
        P("cells"),
        P(),
        P(),
        P(None, AXES),
    )
    out_specs = (P(None, AXES), P(AXES, None))
    return jax.shard_map(
        per_device, mesh=mesh, in_specs=in_specs, out_specs=out_specs, check_vma=False
    )
```

```python
import math

import jax
import jax.numpy as jnp
import numpy as np
from jax import lax
from jax.experimental import pallas as pl
from jax.experimental.pallas import tpu as pltpu
from jax.sharding import PartitionSpec as P

F32, BF16, I32 = jnp.float32, jnp.bfloat16, jnp.int32
AXES = ("cells", "vecs")
LANES = 128
BLOCKS = 8
VMEM_LIMIT = 20 * 2**20


def gll_tables():
    root_value = math.sqrt(3.0 / 7.0)
    points = np.array([-1.0, -root_value, 0.0, root_value, 1.0])
    weights = np.array([0.1, 49.0 / 90.0, 32.0 / 45.0, 49.0 / 90.0, 0.1])
    barycentric = np.ones(5)
    for node_index in range(5):
        for other_node in range(5):
            if other_node != node_index:
                barycentric[node_index] = barycentric[node_index] / (
                    points[node_index] - points[other_node]
                )
    derivative = np.zeros((5, 5))
    for row_index in range(5):
        for col_index in range(5):
            if row_index != col_index:
                derivative[row_index, col_index] = (
                    barycentric[col_index]
                    / barycentric[row_index]
                    / (points[row_index] - points[col_index])
                )
        derivative[row_index, row_index] = -np.sum(derivative[row_index])
    mass_one = np.zeros((5, 5))
    for node_index in range(5):
        mass_one[node_index, node_index] = weights[node_index]
    laplace_one = derivative.T @ mass_one @ derivative
    stiffness = (
        np.kron(np.kron(laplace_one, mass_one), mass_one)
        + np.kron(np.kron(mass_one, laplace_one), mass_one)
        + np.kron(np.kron(mass_one, mass_one), laplace_one)
    )
    quadrature = np.kron(np.kron(weights, weights), weights)
    return (stiffness.astype(np.float32), quadrature.astype(np.float32))


STIFFNESS, QUADRATURE = gll_tables()
STIFFNESS = STIFFNESS.astype(jnp.bfloat16).astype(np.float32)


def node(a, b, c):
    return 25 * a + 5 * b + c


def lane_index(rows):
    return lax.broadcasted_iota(I32, (rows, LANES), 1)


def axis_bits(lane, axis):
    return [(lane >> bit) & 1 for bit in ((0, 3, 5), (1, 4, 6))[axis]]


def axis_place(lane, axis):
    low, mid, high = axis_bits(lane, axis)
    return low + 2 * mid + 4 * high


def below_of(lane, axis):
    low, mid, high = axis_bits(lane, axis)
    scale = 1 + axis
    step = jnp.where(low == 1, 1, jnp.where(mid == 1, 7, 23)) * scale
    first = axis_place(lane, axis) == 0
    return jnp.where(first, lane, lane - step), jnp.logical_not(first)


def above_of(lane, axis):
    low, mid, high = axis_bits(lane, axis)
    scale = 1 + axis
    step = jnp.where(low == 0, 1, jnp.where(mid == 0, 7, 23)) * scale
    last = axis_place(lane, axis) == 7
    return jnp.where(last, lane, lane + step), jnp.logical_not(last)


def pick(values, index):
    return jnp.take_along_axis(values, index, axis=1)


def up_layer(values):
    return pltpu.roll(values, 4, 1)


def down_layer(values):
    return pltpu.roll(values, LANES - 4, 1)


def split_low(values):
    high = values.astype(BF16)
    return high, (values - high.astype(F32)).astype(BF16)


class Nodes:
    def __init__(self, low, mid, top):
        self.low, self.mid, self.top = low, mid, top

    def at(self, j):
        ab, c = divmod(j, 5)
        if c == 0:
            return self.low, ab
        if c == 4:
            return self.top, ab
        return self.mid, 3 * ab + c - 1

    def load(self, j, part=slice(None)):
        ref, row = self.at(j)
        return ref[row, part, :]

    def store(self, j, value, part=slice(None)):
        ref, row = self.at(j)
        ref[row, part, :] = value

    def line(self, j):
        ref, row = self.at(j)
        return ref[row : row + 1, :]

    def store_line(self, j, value):
        ref, row = self.at(j)
        ref[row : row + 1, :] = value


ALL_ROWS = list(range(125))
MID_ROWS = [j for j in ALL_ROWS if j % 5 in (1, 2, 3)]
LOW_ROWS = [j for j in ALL_ROWS if j % 5 == 0]
TOP_ROWS = [j for j in ALL_ROWS if j % 5 == 4]


def upper_lanes(rows):
    return (lane_index(rows) >> 2) & 1 == 1


def one_hot(slots, width):
    place = lax.broadcasted_iota(I32, (256, width), 0).astype(F32).astype(BF16)
    within = jnp.broadcast_to((slots & 255).astype(F32).astype(BF16), (256, width))
    return jnp.where(place == within, BF16(1), BF16(0))


AXIS_MASK = (1 + 8 + 32, 2 + 16 + 64)


def place_bits(place, axis):
    return [(place & 1) + (place & 2) * 4 + (place & 4) * 8, (place & 1) * 2 + (place & 2) * 8 + (place & 4) * 16][axis]


def tile_plan(layers):
    tiles = [("all", [node(a, b, c)]) for a in range(4) for b in range(4) for c in layers]
    for axis in range(2):
        rows = [
            node(4, k, c) if axis == 0 else node(k, 4, c)
            for k in range(5 - axis)
            for c in layers
        ]
        tiles += [(axis, rows[i : i + 8]) for i in range(0, len(rows), 8)]
    return tiles


MID_PLAN, TOP_PLAN = tile_plan((1, 2, 3)), tile_plan((4,))


def tile_groups(plan):
    count = len(plan)
    fives = count % 4
    sizes = [5] * fives + [4] * ((count - 5 * fives) // 4)
    starts = np.cumsum([0] + sizes)
    return [(int(start), size) for start, size in zip(starts, sizes)]


def pack_tile(kind, rows, load, empty):
    if kind == "all":
        return load(rows[0])
    lane = lane_index(8)
    place, last = axis_place(lane, kind), lane | AXIS_MASK[kind]
    tile = jnp.full((8, LANES), empty)
    for i, j in enumerate(rows):
        tile = jnp.where(place == i, pick(load(j), last), tile)
    return tile


def repeated_places(kind, rows):
    return [i for i, j in enumerate(rows) if kind == 0 and j // 5 == 24]


def pack_slots(plan, conn, slots):
    def load(j):
        return jnp.broadcast_to(conn[j : j + 1, :], (8, LANES))

    for i, (kind, rows) in enumerate(plan):
        tile = pack_tile(kind, rows, load, jnp.int32(65535))
        slots[i : i + 1, :] = tile[0:1, :]


def unpack_tiles(plan, extra, load, store):
    lane = lane_index(8)
    for axis in (1, 0):
        after, has_after = above_of(lane, axis)
        for i, (kind, rows) in enumerate(plan):
            if kind != axis:
                continue
            tile = extra(i)
            for place, j in enumerate(rows):
                source = (lane & ~AXIS_MASK[axis]) | place_bits(place, axis)
                inner = pick(load(j - (100 if axis == 0 else 20)), after)
                store(j, jnp.where(has_after, inner, pick(tile, source)))


def gather_rows(vectors, groups, plan, row_of, slots_ref, table, wave, mass, wave_extra, mass_extra):
    base = vectors * groups
    whole = sum(kind == "all" for kind, _ in plan)
    for start, count in tile_groups(plan):
        width = count * LANES
        slots = jnp.concatenate([slots_ref[start + i : start + i + 1, :] for i in range(count)], 1)
        chosen = one_hot(slots, width)
        found = jnp.dot(
            table[...], jnp.concatenate([chosen, chosen], 0), preferred_element_type=F32
        )
        group = slots >> 8
        wide = jnp.broadcast_to(group, (vectors, width))
        total = jnp.zeros((vectors, width), F32)
        for h in range(groups):
            total = jnp.where(wide == h, found[vectors * h : vectors * (h + 1)], total)
        group_row = lax.broadcasted_iota(I32, (groups, width), 0)
        mine = group_row == jnp.broadcast_to(group, (groups, width))
        line = jnp.sum(jnp.where(mine, found[base : base + groups], 0.0), 0, keepdims=True)
        for i in range(count):
            kind, rows = plan[start + i]
            columns = slice(LANES * i, LANES * (i + 1))
            if kind == "all":
                row = row_of(rows[0])
                wave[row] = total[:, columns]
                mass[row : row + 1, :] = line[:, columns]
            else:
                wave_extra[start + i - whole] = total[:, columns]
                mass_extra[start + i - whole] = jnp.broadcast_to(line[:, columns], (8, LANES))
    for half in range(vectors // 8):
        part = slice(8 * half, 8 * (half + 1))

        def store(j, value):
            wave[row_of(j), part, :] = value

        unpack_tiles(
            plan, lambda i: wave_extra[i - whole, part, :], lambda j: wave[row_of(j), part, :], store
        )

    def store_line(j, value):
        mass[row_of(j) : row_of(j) + 1, :] = value[0:1, :]

    def load_line(j):
        return jnp.broadcast_to(mass[row_of(j) : row_of(j) + 1, :], (8, LANES))

    unpack_tiles(plan, lambda i: mass_extra[i - whole], load_line, store_line)


def mid_row(j):
    return 3 * (j // 5) + j % 5 - 1


def top_row(j):
    return j // 5


def gather_face_kernel(
    vectors, conn_hbm, wave_hbm, mass_hbm, table, conn, slots, wave_top, mass_top, face_out,
    wave_in, mass_in, wave_extra, mass_extra, sems,
):
    copies = [
        pltpu.make_async_copy(conn_hbm, conn, sems.at[2]),
        pltpu.make_async_copy(wave_hbm, wave_in, sems.at[0]),
        pltpu.make_async_copy(mass_hbm, mass_in, sems.at[1]),
    ]
    for copy in copies:
        copy.start()
    copies[0].wait()
    pack_slots(TOP_PLAN, conn, slots)
    for copy in copies[1:]:
        copy.wait()
    groups = wave_in.shape[1] // 256
    base = vectors * groups
    high, low = split_low(wave_in[...])
    for h in range(groups):
        table[vectors * h : vectors * (h + 1), 0:256] = high[:, 256 * h : 256 * (h + 1)]
        table[vectors * h : vectors * (h + 1), 256:512] = low[:, 256 * h : 256 * (h + 1)]
    for half in range(2):
        high, low = split_low(mass_in[pl.ds(half, groups, stride=2), :])
        spare = jnp.zeros((table.shape[0] - base - groups, LANES), F32)
        columns = slice(LANES * half, LANES * (half + 1))
        table[base:, columns] = jnp.concatenate([high.astype(F32), spare], 0).astype(BF16)
        columns = slice(256 + LANES * half, 256 + LANES * (half + 1))
        table[base:, columns] = jnp.concatenate([low.astype(F32), spare], 0).astype(BF16)
    gather_rows(
        vectors, groups, TOP_PLAN, top_row, slots, table, wave_top, mass_top, wave_extra, mass_extra
    )
    upper, upper_one = upper_lanes(vectors), upper_lanes(1)
    for i in range(13):
        second = min(2 * i + 1, 24)
        face_out[i, 0:vectors, :] = jnp.where(upper, wave_top[2 * i], down_layer(wave_top[second]))
        packed = jnp.where(
            upper_one,
            mass_top[2 * i : 2 * i + 1, :],
            down_layer(mass_top[second : second + 1, :]),
        )
        face_out[i, vectors : vectors + 8, :] = jnp.broadcast_to(packed, (8, LANES))


def gather_rest_kernel(
    vectors, groups, table, conn, potential_hbm, levels_hbm, constants,
    slots, wave_mid, mass_mid, kinetic, coefficient, levels_in, wave_extra, mass_extra, sems,
):
    copies = [
        pltpu.make_async_copy(potential_hbm, coefficient, sems.at[0]),
        pltpu.make_async_copy(levels_hbm, levels_in, sems.at[1]),
    ]
    for copy in copies:
        copy.start()
    pack_slots(MID_PLAN, conn, slots)
    gather_rows(
        vectors, groups, MID_PLAN, mid_row, slots, table, wave_mid, mass_mid, wave_extra, mass_extra
    )
    for copy in copies:
        copy.wait()
    size = jnp.exp2(-levels_in[...].astype(F32))
    in_use = jnp.where(lane_index(1).astype(F32) < constants[2:3, :], 1.0, 0.0)
    kinetic[...] = jnp.broadcast_to(size / 4.0 * in_use, (8, LANES))
    volume = size * size * size / 8.0 * in_use
    for j in ALL_ROWS:
        line = volume * float(QUADRATURE[j]) * coefficient[j : j + 1, :]
        coefficient[j : j + 1, :] = line


def apply_cells(values, terms, kinetic, coefficient, rows, vectors):
    def one(t, carry):
        part = pl.ds(pl.multiple_of(8 * t, 8), 8)
        for j in rows:
            total = None
            for k in np.flatnonzero(STIFFNESS[j]):
                term = values[int(k), part, :] * float(STIFFNESS[j, k])
                total = term if total is None else total + term
            weight = jnp.broadcast_to(coefficient[j : j + 1, :], (8, LANES))
            terms.store(j, kinetic[...] * total + weight * values[j, part, :], part)
        return carry

    lax.fori_loop(0, vectors // 8, one, 0)


def join_layer(terms, layers, vectors):
    lane = lane_index(8)
    moves = [below_of(lane, axis) + above_of(lane, axis) for axis in range(2)]

    def one(t, carry):
        part = pl.ds(pl.multiple_of(8 * t, 8), 8)
        for axis in range(2):
            before, has_before, after, has_after = moves[axis]
            for other in range(5):
                for c in layers:
                    start = node(0, other, c) if axis == 0 else node(other, 0, c)
                    end = node(4, other, c) if axis == 0 else node(other, 4, c)
                    first, last = terms.load(start, part), terms.load(end, part)
                    joined = first + jnp.where(has_before, pick(last, before), 0.0)
                    terms.store(start, joined, part)
                    terms.store(end, jnp.where(has_after, pick(joined, after), last), part)
        return carry

    lax.fori_loop(0, vectors // 8, one, 0)


def pack_lower(low, face_out, vectors):
    upper = upper_lanes(vectors)
    for i in range(13):
        second = min(2 * i + 1, 24)
        face_out[i] = jnp.where(upper, up_layer(low[second]), low[2 * i]).astype(BF16)


def pack_upper(top, face_out, vectors):
    upper = upper_lanes(vectors)
    for i in range(13):
        second = min(2 * i + 1, 24)
        face_out[i] = jnp.where(upper, top[2 * i], down_layer(top[second])).astype(BF16)


def from_below(packed, ab):
    return packed if ab % 2 == 1 else down_layer(packed)


def from_above(packed, ab):
    return packed if ab % 2 == 1 else up_layer(packed)


def first_faces_kernel(
    vectors, wave_mid, wave_top, mass_mid, mass_top, ghost, kinetic, coefficient,
    values, wave_low, mass_low, low, top, face_down, face_up,
):
    upper, upper_one = upper_lanes(vectors), upper_lanes(1)
    for ab in range(25):
        packed = ghost[ab // 2]
        wave_low[ab] = jnp.where(upper, up_layer(wave_top[ab]), from_below(packed[0:vectors], ab))
        mass_low[ab : ab + 1, :] = jnp.where(
            upper_one,
            up_layer(mass_top[ab : ab + 1, :]),
            from_below(packed[vectors : vectors + 1], ab),
        )
    wave, mass = Nodes(wave_low, wave_mid, wave_top), Nodes(mass_low, mass_mid, mass_top)
    for j in ALL_ROWS:
        values[j] = (wave.load(j) * mass.line(j)).astype(BF16).astype(F32)
    terms = Nodes(low, None, top)
    apply_cells(values, terms, kinetic, coefficient, LOW_ROWS + TOP_ROWS, vectors)
    join_layer(terms, (0, 4), vectors)
    pack_lower(low, face_down, vectors)
    pack_upper(top, face_up, vectors)


def rest_kernel(vectors, values, kinetic, coefficient, mid):
    terms = Nodes(None, mid, None)
    apply_cells(values, terms, kinetic, coefficient, MID_ROWS, vectors)
    join_layer(terms, (1, 2, 3), vectors)


def second_faces_kernel(
    vectors, low, mid, top, wave_low, wave_mid, wave_top, mass_low, mass_mid, mass_top,
    above, below, kinetic, coefficient, constants,
    values, base_mid, base_top, low_out, face_down,
):
    upper = upper_lanes(vectors)
    center, inverse = constants[0:1, :], constants[1:2, :]
    again = (-2.0 * center) * inverse
    sums = Nodes(low, mid, top)
    wave, mass = Nodes(wave_low, wave_mid, wave_top), Nodes(mass_low, mass_mid, mass_top)
    base = Nodes(None, base_mid, base_top)

    def degree_one(j, total):
        one = (mass.line(j) * total - center * wave.load(j)) * inverse
        values[j] = (one * mass.line(j)).astype(BF16).astype(F32)
        if j % 5 > 0:
            base.store(j, again * one - wave.load(j))

    for ab in range(25):
        first, last = low[ab], top[ab]
        shared = first + up_layer(last)
        incoming = from_below(below[ab // 2].astype(F32), ab)
        degree_one(5 * ab, jnp.where(upper, shared, first + incoming))
        incoming = from_above(above[ab // 2].astype(F32), ab)
        degree_one(5 * ab + 4, jnp.where(upper, last + incoming, down_layer(shared)))
        for c in range(1, 4):
            degree_one(5 * ab + c, mid[3 * ab + c - 1])
    terms = Nodes(low_out, None, None)
    apply_cells(values, terms, kinetic, coefficient, LOW_ROWS, vectors)
    join_layer(terms, (0,), vectors)
    pack_lower(low_out, face_down, vectors)


def scatter_rows(vectors, groups, plan, slots_ref, load, total):
    for start, count in tile_groups(plan):
        width = count * LANES
        pieces = []
        for kind, rows in plan[start : start + count]:
            halves = []
            for half in range(vectors // 8):
                part = slice(8 * half, 8 * (half + 1))
                halves.append(pack_tile(kind, rows, lambda j: load(j, part), jnp.float32(0)))
            pieces.append(jnp.concatenate(halves, 0).astype(BF16))
        value = jnp.concatenate(pieces, 1)
        slots = []
        for i in range(count):
            slot = slots_ref[start + i : start + i + 1, :]
            for place in repeated_places(*plan[start + i]):
                lane = lane_index(1)
                again = jnp.logical_and(axis_place(lane, 0) == place, axis_place(lane, 1) < 7)
                slot = jnp.where(again, 65535, slot)
            slots.append(slot)
        slot = jnp.concatenate(slots, 1)
        group = slot >> 8
        wide = jnp.broadcast_to(group.astype(F32).astype(BF16), (vectors, width))
        spread = [jnp.where(wide == BF16(h), value, BF16(0)) for h in range(groups)]
        spare = total.shape[0] - vectors * groups
        group_row = lax.broadcasted_iota(I32, (spare, width), 0)
        held = jnp.where(group_row == jnp.broadcast_to(group, (spare, width)), 1.0, 0.0)
        spread.append(held.astype(BF16))
        moved = lax.dot_general(
            jnp.concatenate(spread, 0),
            one_hot(slot, width),
            (((1,), (1,)), ((), ())),
            preferred_element_type=F32,
        )
        if start == 0:
            total[...] = moved
        else:
            total[...] += moved


def second_rest_kernel(
    vectors, values, kinetic, coefficient, low, mass_mid, mass_top, base_mid, base_top, slots,
    wave_hbm, earlier_hbm, constants,
    total, done_top, alone, *rest,
):
    earlier, (mid, top, wave_in, sems) = rest[:-4], rest[-4:]
    copy = pltpu.make_async_copy(wave_hbm, wave_in, sems.at[0])
    copy.start()
    loads = []
    for i, part in enumerate(earlier):
        size = part.shape[0]
        source = earlier_hbm.at[size * i : size * (i + 1), :]
        loads.append(pltpu.make_async_copy(source, part, sems.at[1 + i]))
        loads[-1].start()
    groups = wave_in.shape[1] // 256
    center, inverse = constants[0:1, :], constants[1:2, :]
    terms = Nodes(None, mid, top)
    apply_cells(values, terms, kinetic, coefficient, MID_ROWS + TOP_ROWS, vectors)
    join_layer(terms, (1, 2, 3, 4), vectors)
    upper = upper_lanes(vectors)
    for ab in range(25):
        last = top[ab]
        joined = jnp.where(upper, last, down_layer(low[ab]) + last)
        line = (2.0 * inverse) * mass_top[ab : ab + 1, :]
        done_top[ab] = base_top[ab] + line * joined

    def load(j, part):
        row = mid_row(j)
        line = (2.0 * inverse) * mass_mid[row : row + 1, :]
        return base_mid[row, part, :] + line * mid[row, part, :]

    scatter_rows(vectors, groups, MID_PLAN, slots, load, total)
    copy.wait()
    wide_inverse = jnp.concatenate([inverse, inverse], 1)
    wide_center = jnp.concatenate([center, center], 1)
    for h in range(groups):
        wave = wave_in[:, 256 * h : 256 * (h + 1)]
        one = -wide_center * wave * wide_inverse
        alone[:, 256 * h : 256 * (h + 1)] = (
            (-2.0 * wide_center) * wide_inverse * one - wave
        ).astype(BF16)
    for load in loads:
        load.wait()


def scatter_top_kernel(
    vectors, slots, before, done_top, mass_top, above, alone, constants, *rest
):
    outs, (placed, total) = rest[:-2], rest[-2:]
    groups = alone.shape[1] // 256
    base = vectors * groups
    upper = upper_lanes(8)
    inverse = constants[1:2, :]

    def load(j, part):
        ab = j // 5
        incoming = from_above(above[ab // 2].astype(F32)[part], ab)
        share = (2.0 * inverse) * mass_top[ab : ab + 1, :] * incoming
        return done_top[ab, part, :] + jnp.where(upper, share, 0.0)

    scatter_rows(vectors, groups, TOP_PLAN, slots, load, total)
    parts, part = len(outs), lax.axis_index("vecs")
    quarter = groups // parts
    for h in range(groups):
        rows = slice(vectors * h, vectors * (h + 1))
        count = total[base + h : base + h + 1, :] + before[base + h : base + h + 1, :]
        value = total[rows, :] + before[rows, :]
        own = alone[:, 256 * h : 256 * (h + 1)].astype(F32)
        at = h % quarter
        away = lax.rem(h // quarter + parts - part, parts)
        placed[away, :, 256 * at : 256 * (at + 1)] = jnp.where(count > 0.5, value, own).astype(BF16)
    for away, out in enumerate(outs):
        out[...] = placed[away]


def earlier_rows(earlier, start, size):
    pieces, height = [], earlier[0].shape[0]
    while size > 0:
        block, at = divmod(start, height)
        count = min(size, height - at)
        pieces.append(earlier[block][at : at + count, :])
        start, size = start + count, size - count
    return pieces


def project_kernel(cores, parts, share, other, quarter, *rest):
    earlier, (out,) = rest[:-1], rest[-1:]
    half, block = share // 2, parts * share
    total = sum(part.shape[0] for part in earlier)
    here = lax.rem(lax.axis_index("cells"), cores)
    for core in range(cores):

        @pl.when(here == (1 - core if other else core))
        def _():
            pieces = []
            for start in range(core * block, total, cores * block):
                pieces += earlier_rows(earlier, start, block)
            product = lax.dot_general(
                jnp.concatenate(pieces, 0),
                quarter[...],
                (((1,), (1,)), ((), ())),
                preferred_element_type=F32,
            )
            product = product.reshape(out.shape[0], share, product.shape[-1])
            out[...] = jnp.concatenate([product[:, :half], product[:, half:]], 2)


def gather_pieces_kernel(parts, *refs):
    quarter = refs[-1]
    for away, piece in enumerate(refs[:-1]):
        size = piece.shape[0]
        source = lax.rem(lax.axis_index("vecs") + parts - away, parts)
        quarter[pl.ds(pl.multiple_of(size * source, size), size), :] = piece[...]


def pair_sum_kernel(keep, received, out):
    out[...] = (keep[...] + received[...]).astype(out.dtype)


def own_rows_kernel(shares, own_rows, spread):
    own = jnp.sum(shares[...].astype(F32), 0)
    columns = own.shape[1] // 2
    own_rows[...] = jnp.concatenate([own[:, :columns], own[:, columns:]], 0)
    spread[...] = jnp.broadcast_to(own[None], spread.shape).astype(BF16)


def filter_kernel(cores, parts, share, mine, theirs, quarter, *rest):
    earlier, (out_ref, low) = rest[:-2], rest[-2:]
    half = share // 2
    columns = mine.shape[-1] // 2
    block = parts * share

    def unpack(ref, core):
        value = ref[...].astype(F32)
        value = jnp.concatenate([value[:, :, :columns], value[:, :, columns:]], 1)
        value = value.reshape(value.shape[0] // parts, block, columns)
        for i in range(value.shape[0]):
            at = (cores * i + core) * block
            low[at : at + block, :] = value[i].astype(BF16)

    for core in range(cores):

        @pl.when(lax.rem(lax.axis_index("cells"), cores) == core)
        def _():
            unpack(mine, core)
            unpack(theirs, 1 - core)

    width = 256
    for i in range(out_ref.shape[1] // width):
        at = slice(width * i, width * (i + 1))
        product = lax.dot_general(
            low[...],
            jnp.concatenate([part[:, at] for part in earlier], 0),
            (((0,), (0,)), ((), ())),
            preferred_element_type=F32,
        )
        out_ref[:, at] = quarter[:, at].astype(F32) - product


VMEM_SPEC = pl.BlockSpec(memory_space=pltpu.VMEM)
HBM_SPEC = pl.BlockSpec(memory_space=pltpu.HBM)


def call(kernel, name, out_shape, specs, scratch, *operands):
    return pl.pallas_call(
        kernel,
        out_shape=out_shape,
        in_specs=[{"v": VMEM_SPEC, "h": HBM_SPEC}[letter] for letter in specs],
        out_specs=jax.tree.map(lambda _: VMEM_SPEC, out_shape),
        scratch_shapes=scratch,
        compiler_params=pltpu.CompilerParams(vmem_limit_bytes=VMEM_LIMIT),
        name=name,
    )(*[
        pltpu.with_memory_space_constraint(operand, pltpu.HBM) if letter == "h" else operand
        for letter, operand in zip(specs, operands)
    ])


def passed_along(value, axis, steps):
    count = lax.axis_size(axis)
    leading, last = (max(0, -steps), min(count, count - steps))
    return lax.ppermute(value, axis, [(source, source + steps) for source in range(leading, last)])


def per_device(
    wave_block, connectivity, send_list, levels, live_cells, potential, mass_scale,
    center, halfwidth, earlier_vectors,
):
    vectors, owned = wave_block.shape
    groups = owned // 256
    table_rows = vectors * groups + 48
    cells, parts = lax.axis_size("cells"), lax.axis_size("vecs")
    devices, cores = cells * parts, 2
    turn = lambda away: [(i, (i + away) % parts) for i in range(parts)]
    line = lax.broadcasted_iota(I32, (8, LANES), 0)
    constants = jnp.where(line == 1, 1.0 / halfwidth, live_cells[0].astype(F32))
    constants = jnp.where(line == 0, center, constants)

    def shape(*sizes, kind=F32):
        return jax.ShapeDtypeStruct(sizes, kind)

    def rows(count):
        return shape(count, vectors, LANES)

    def lines(count):
        return shape(count, LANES)

    packed = shape(13, vectors, LANES, kind=BF16)
    scratch_rows = lambda count: pltpu.VMEM((count, vectors, LANES), F32)
    wave_scratch = pltpu.VMEM((vectors, owned), F32)

    extra = lambda count: [scratch_rows(count), pltpu.VMEM((count, 8, LANES), F32)]
    table, conn, slots_top, wave_top, mass_top, face = call(
        lambda *refs: gather_face_kernel(vectors, *refs),
        "gather_face",
        (
            shape(table_rows, 512, kind=BF16), shape(125, LANES, kind=I32),
            shape(len(TOP_PLAN), LANES, kind=I32), rows(25), lines(25),
            shape(13, vectors + 8, LANES),
        ),
        "hhh",
        [wave_scratch, pltpu.VMEM((owned // LANES, LANES), F32), *extra(2), pltpu.SemaphoreType.DMA((3,))],
        connectivity, wave_block, mass_scale.reshape(owned // LANES, LANES),
    )
    ghost = passed_along(face, "cells", 1)
    slots_mid, wave_mid, mass_mid, kinetic, coefficient = call(
        lambda *refs: gather_rest_kernel(vectors, groups, *refs),
        "gather_rest",
        (
            shape(len(MID_PLAN), LANES, kind=I32), rows(75), lines(75), lines(8), lines(125),
        ),
        "vvhhv",
        [
            pltpu.VMEM((1, LANES), I32), *extra(4), pltpu.SemaphoreType.DMA((2,)),
        ],
        table, conn, potential, levels.reshape(1, LANES), constants,
    )
    values, wave_low, mass_low, low, top, face_down, face_up = call(
        lambda *refs: first_faces_kernel(vectors, *refs),
        "first_faces",
        (rows(125), rows(25), lines(25), rows(25), rows(25), packed, packed),
        "vvvvvvv",
        [],
        wave_mid, wave_top, mass_mid, mass_top, ghost, kinetic, coefficient,
    )
    above = passed_along(face_down, "cells", -1)
    below = passed_along(face_up, "cells", 1)
    mid = call(
        lambda *refs: rest_kernel(vectors, *refs), "first_rest", rows(75), "vvv", [],
        values, kinetic, coefficient,
    )
    values, base_mid, base_top, low, face_down = call(
        lambda *refs: second_faces_kernel(vectors, *refs),
        "second_faces",
        (rows(125), rows(75), rows(25), rows(25), packed),
        "v" * 14,
        [],
        low, mid, top, wave_low, wave_mid, wave_top, mass_low, mass_mid, mass_top,
        above, below, kinetic, coefficient, constants,
    )
    above = passed_along(face_down, "cells", -1)
    before, done_top, alone, *earlier = call(
        lambda *refs: second_rest_kernel(vectors, *refs),
        "second_rest",
        (
            shape(table_rows, 256), rows(25), shape(vectors, owned, kind=BF16),
            *[shape(earlier_vectors.shape[0] // BLOCKS, owned // parts, kind=BF16)] * BLOCKS,
        ),
        "v" * 9 + "hhv",
        [scratch_rows(75), scratch_rows(25), wave_scratch, pltpu.SemaphoreType.DMA((1 + BLOCKS,))],
        values, kinetic, coefficient, low, mass_mid, mass_top, base_mid, base_top, slots_mid,
        wave_block, earlier_vectors, constants,
    )
    pieces = call(
        lambda *refs: scatter_top_kernel(vectors, *refs),
        "scatter_top",
        (shape(vectors, owned // parts, kind=BF16),) * parts,
        "vvvvvvv",
        [pltpu.VMEM((parts, vectors, owned // parts), BF16), pltpu.VMEM((table_rows, 256), F32)],
        slots_top, before, done_top, mass_top, above, alone, constants,
    )
    pieces = [
        lax.ppermute(piece, "vecs", turn(away)) if away else piece
        for away, piece in enumerate(pieces)
    ]
    total_vectors = parts * vectors
    share = earlier_vectors.shape[0] // devices
    half, peers = share // 2, devices // cores
    pair = [(i, i ^ 1) for i in range(cells)]
    same_core = [
        [(cores * block + k) * parts + part for block in range(cells // cores) for part in range(parts)]
        for k in range(cores)
    ]
    sent = shape(peers, half, 2 * total_vectors)
    quarter = call(
        lambda *refs: gather_pieces_kernel(parts, *refs),
        "gather_pieces",
        shape(total_vectors, owned // parts, kind=BF16),
        "v" * parts, [], *pieces,
    )
    send, keep = [
        call(
            lambda *refs, other=other: project_kernel(cores, parts, share, other, *refs),
            "project_other" if other else "project_own",
            sent, "v" * (1 + BLOCKS), [], quarter, *earlier,
        )
        for other in (True, False)
    ]
    shares = call(
        pair_sum_kernel, "pair_sum", shape(*sent.shape, kind=BF16), "vv", [],
        keep, lax.ppermute(send, "cells", pair),
    )
    shares = lax.all_to_all(
        shares, AXES, split_axis=0, concat_axis=0, tiled=True, axis_index_groups=same_core
    )
    own_rows, mine = call(
        own_rows_kernel,
        "own_rows",
        (shape(share, total_vectors), shape(peers, half, 2 * total_vectors, kind=BF16)),
        "v", [], shares,
    )
    mine = lax.all_to_all(
        mine, AXES, split_axis=0, concat_axis=0, tiled=True, axis_index_groups=same_core
    )
    theirs = lax.ppermute(mine, "cells", pair)
    filtered = call(
        lambda *refs: filter_kernel(cores, parts, share, *refs),
        "filter",
        shape(total_vectors, owned // parts),
        "vvv" + "v" * BLOCKS,
        [pltpu.VMEM((devices * share, total_vectors), BF16)],
        mine, theirs, quarter, *earlier,
    )
    return (filtered, own_rows)


def solution(mesh):
    in_specs = (
        P("vecs", "cells"),
        P(None, "cells"),
        P("cells"),
        P("cells"),
        P("cells"),
        P(None, "cells"),
        P("cells"),
        P(),
        P(),
        P(None, AXES),
    )
    out_specs = (P(None, AXES), P(AXES, None))
    return jax.shard_map(
        per_device, mesh=mesh, in_specs=in_specs, out_specs=out_specs, check_vma=False
    )
```

```python
import math

import jax
import jax.numpy as jnp
import numpy as np
from jax import lax
from jax.experimental import pallas as pl
from jax.experimental.pallas import tpu as pltpu
from jax.sharding import PartitionSpec as P

F32, BF16, I32 = jnp.float32, jnp.bfloat16, jnp.int32
AXES = ("cells", "vecs")
LANES = 128
BLOCKS = 8
VMEM_LIMIT = 20 * 2**20


def gll_tables():
    root_value = math.sqrt(3.0 / 7.0)
    points = np.array([-1.0, -root_value, 0.0, root_value, 1.0])
    weights = np.array([0.1, 49.0 / 90.0, 32.0 / 45.0, 49.0 / 90.0, 0.1])
    barycentric = np.ones(5)
    for node_index in range(5):
        for other_node in range(5):
            if other_node != node_index:
                barycentric[node_index] = barycentric[node_index] / (
                    points[node_index] - points[other_node]
                )
    derivative = np.zeros((5, 5))
    for row_index in range(5):
        for col_index in range(5):
            if row_index != col_index:
                derivative[row_index, col_index] = (
                    barycentric[col_index]
                    / barycentric[row_index]
                    / (points[row_index] - points[col_index])
                )
        derivative[row_index, row_index] = -np.sum(derivative[row_index])
    mass_one = np.zeros((5, 5))
    for node_index in range(5):
        mass_one[node_index, node_index] = weights[node_index]
    laplace_one = derivative.T @ mass_one @ derivative
    stiffness = (
        np.kron(np.kron(laplace_one, mass_one), mass_one)
        + np.kron(np.kron(mass_one, laplace_one), mass_one)
        + np.kron(np.kron(mass_one, mass_one), laplace_one)
    )
    quadrature = np.kron(np.kron(weights, weights), weights)
    return (stiffness.astype(np.float32), quadrature.astype(np.float32))


STIFFNESS, QUADRATURE = gll_tables()
STIFFNESS = STIFFNESS.astype(jnp.bfloat16).astype(np.float32)


def node(a, b, c):
    return 25 * a + 5 * b + c


def lane_index(rows):
    return lax.broadcasted_iota(I32, (rows, LANES), 1)


def axis_bits(lane, axis):
    return [(lane >> bit) & 1 for bit in ((0, 3, 5), (1, 4, 6))[axis]]


def axis_place(lane, axis):
    low, mid, high = axis_bits(lane, axis)
    return low + 2 * mid + 4 * high


def below_of(lane, axis):
    low, mid, high = axis_bits(lane, axis)
    scale = 1 + axis
    step = jnp.where(low == 1, 1, jnp.where(mid == 1, 7, 23)) * scale
    first = axis_place(lane, axis) == 0
    return jnp.where(first, lane, lane - step), jnp.logical_not(first)


def above_of(lane, axis):
    low, mid, high = axis_bits(lane, axis)
    scale = 1 + axis
    step = jnp.where(low == 0, 1, jnp.where(mid == 0, 7, 23)) * scale
    last = axis_place(lane, axis) == 7
    return jnp.where(last, lane, lane + step), jnp.logical_not(last)


def pick(values, index):
    return jnp.take_along_axis(values, index, axis=1)


def up_layer(values):
    return pltpu.roll(values, 4, 1)


def down_layer(values):
    return pltpu.roll(values, LANES - 4, 1)


def split_low(values):
    high = values.astype(BF16)
    return high, (values - high.astype(F32)).astype(BF16)


class Nodes:
    def __init__(self, low, mid, top):
        self.low, self.mid, self.top = low, mid, top

    def at(self, j):
        ab, c = divmod(j, 5)
        if c == 0:
            return self.low, ab
        if c == 4:
            return self.top, ab
        return self.mid, 3 * ab + c - 1

    def load(self, j, part=slice(None)):
        ref, row = self.at(j)
        return ref[row, part, :]

    def store(self, j, value, part=slice(None)):
        ref, row = self.at(j)
        ref[row, part, :] = value

    def line(self, j):
        ref, row = self.at(j)
        return ref[row : row + 1, :]

    def store_line(self, j, value):
        ref, row = self.at(j)
        ref[row : row + 1, :] = value


ALL_ROWS = list(range(125))
MID_ROWS = [j for j in ALL_ROWS if j % 5 in (1, 2, 3)]
LOW_ROWS = [j for j in ALL_ROWS if j % 5 == 0]
TOP_ROWS = [j for j in ALL_ROWS if j % 5 == 4]


def upper_lanes(rows):
    return (lane_index(rows) >> 2) & 1 == 1


def one_hot(slots, width):
    place = lax.broadcasted_iota(I32, (256, width), 0).astype(F32).astype(BF16)
    within = jnp.broadcast_to((slots & 255).astype(F32).astype(BF16), (256, width))
    return jnp.where(place == within, BF16(1), BF16(0))


AXIS_MASK = (1 + 8 + 32, 2 + 16 + 64)


def place_bits(place, axis):
    return [(place & 1) + (place & 2) * 4 + (place & 4) * 8, (place & 1) * 2 + (place & 2) * 8 + (place & 4) * 16][axis]


def tile_plan(layers):
    tiles = [("all", [node(a, b, c)]) for a in range(4) for b in range(4) for c in layers]
    for axis in range(2):
        rows = [
            node(4, k, c) if axis == 0 else node(k, 4, c)
            for k in range(5 - axis)
            for c in layers
        ]
        tiles += [(axis, rows[i : i + 8]) for i in range(0, len(rows), 8)]
    return tiles


MID_PLAN, TOP_PLAN = tile_plan((1, 2, 3)), tile_plan((4,))


def tile_groups(plan):
    count = len(plan)
    fives = count % 4
    sizes = [5] * fives + [4] * ((count - 5 * fives) // 4)
    starts = np.cumsum([0] + sizes)
    return [(int(start), size) for start, size in zip(starts, sizes)]


def pack_tile(kind, rows, load, empty):
    if kind == "all":
        return load(rows[0])
    lane = lane_index(8)
    place, last = axis_place(lane, kind), lane | AXIS_MASK[kind]
    tile = jnp.full((8, LANES), empty)
    for i, j in enumerate(rows):
        tile = jnp.where(place == i, pick(load(j), last), tile)
    return tile


def repeated_places(kind, rows):
    return [i for i, j in enumerate(rows) if kind == 0 and j // 5 == 24]


def pack_slots(plan, conn, slots):
    def load(j):
        return jnp.broadcast_to(conn[j : j + 1, :], (8, LANES))

    for i, (kind, rows) in enumerate(plan):
        tile = pack_tile(kind, rows, load, jnp.int32(65535))
        slots[i : i + 1, :] = tile[0:1, :]


def unpack_tiles(plan, extra, load, store):
    lane = lane_index(8)
    for axis in (1, 0):
        after, has_after = above_of(lane, axis)
        for i, (kind, rows) in enumerate(plan):
            if kind != axis:
                continue
            tile = extra(i)
            for place, j in enumerate(rows):
                source = (lane & ~AXIS_MASK[axis]) | place_bits(place, axis)
                inner = pick(load(j - (100 if axis == 0 else 20)), after)
                store(j, jnp.where(has_after, inner, pick(tile, source)))


def gather_rows(vectors, groups, plan, row_of, slots_ref, table, wave, mass, wave_extra, mass_extra):
    base = vectors * groups
    whole = sum(kind == "all" for kind, _ in plan)
    for start, count in tile_groups(plan):
        width = count * LANES
        slots = jnp.concatenate([slots_ref[start + i : start + i + 1, :] for i in range(count)], 1)
        chosen = one_hot(slots, width)
        found = jnp.dot(
            table[...], jnp.concatenate([chosen, chosen], 0), preferred_element_type=F32
        )
        group = slots >> 8
        wide = jnp.broadcast_to(group, (vectors, width))
        total = jnp.zeros((vectors, width), F32)
        for h in range(groups):
            total = jnp.where(wide == h, found[vectors * h : vectors * (h + 1)], total)
        group_row = lax.broadcasted_iota(I32, (groups, width), 0)
        mine = group_row == jnp.broadcast_to(group, (groups, width))
        line = jnp.sum(jnp.where(mine, found[base : base + groups], 0.0), 0, keepdims=True)
        for i in range(count):
            kind, rows = plan[start + i]
            columns = slice(LANES * i, LANES * (i + 1))
            if kind == "all":
                row = row_of(rows[0])
                wave[row] = total[:, columns]
                mass[row : row + 1, :] = line[:, columns]
            else:
                wave_extra[start + i - whole] = total[:, columns]
                mass_extra[start + i - whole] = jnp.broadcast_to(line[:, columns], (8, LANES))
    for half in range(vectors // 8):
        part = slice(8 * half, 8 * (half + 1))

        def store(j, value):
            wave[row_of(j), part, :] = value

        unpack_tiles(
            plan, lambda i: wave_extra[i - whole, part, :], lambda j: wave[row_of(j), part, :], store
        )

    def store_line(j, value):
        mass[row_of(j) : row_of(j) + 1, :] = value[0:1, :]

    def load_line(j):
        return jnp.broadcast_to(mass[row_of(j) : row_of(j) + 1, :], (8, LANES))

    unpack_tiles(plan, lambda i: mass_extra[i - whole], load_line, store_line)


def mid_row(j):
    return 3 * (j // 5) + j % 5 - 1


def top_row(j):
    return j // 5


def gather_face_kernel(
    vectors, conn_hbm, wave_hbm, mass_hbm, table, conn, slots, wave_top, mass_top, face_out,
    wave_in, mass_in, wave_extra, mass_extra, sems,
):
    copies = [
        pltpu.make_async_copy(conn_hbm, conn, sems.at[2]),
        pltpu.make_async_copy(wave_hbm, wave_in, sems.at[0]),
        pltpu.make_async_copy(mass_hbm, mass_in, sems.at[1]),
    ]
    for copy in copies:
        copy.start()
    copies[0].wait()
    pack_slots(TOP_PLAN, conn, slots)
    for copy in copies[1:]:
        copy.wait()
    groups = wave_in.shape[1] // 256
    base = vectors * groups
    high, low = split_low(wave_in[...])
    for h in range(groups):
        table[vectors * h : vectors * (h + 1), 0:256] = high[:, 256 * h : 256 * (h + 1)]
        table[vectors * h : vectors * (h + 1), 256:512] = low[:, 256 * h : 256 * (h + 1)]
    for half in range(2):
        high, low = split_low(mass_in[pl.ds(half, groups, stride=2), :])
        spare = jnp.zeros((table.shape[0] - base - groups, LANES), F32)
        columns = slice(LANES * half, LANES * (half + 1))
        table[base:, columns] = jnp.concatenate([high.astype(F32), spare], 0).astype(BF16)
        columns = slice(256 + LANES * half, 256 + LANES * (half + 1))
        table[base:, columns] = jnp.concatenate([low.astype(F32), spare], 0).astype(BF16)
    gather_rows(
        vectors, groups, TOP_PLAN, top_row, slots, table, wave_top, mass_top, wave_extra, mass_extra
    )
    upper, upper_one = upper_lanes(vectors), upper_lanes(1)
    for i in range(13):
        second = min(2 * i + 1, 24)
        face_out[i, 0:vectors, :] = jnp.where(upper, wave_top[2 * i], down_layer(wave_top[second]))
        packed = jnp.where(
            upper_one,
            mass_top[2 * i : 2 * i + 1, :],
            down_layer(mass_top[second : second + 1, :]),
        )
        face_out[i, vectors : vectors + 8, :] = jnp.broadcast_to(packed, (8, LANES))


def gather_rest_kernel(
    vectors, groups, table, conn, potential_hbm, levels_hbm, live_ref,
    slots, wave_mid, mass_mid, kinetic, coefficient, levels_in, wave_extra, mass_extra, sems,
):
    copies = [
        pltpu.make_async_copy(potential_hbm, coefficient, sems.at[0]),
        pltpu.make_async_copy(levels_hbm, levels_in, sems.at[1]),
    ]
    for copy in copies:
        copy.start()
    pack_slots(MID_PLAN, conn, slots)
    gather_rows(
        vectors, groups, MID_PLAN, mid_row, slots, table, wave_mid, mass_mid, wave_extra, mass_extra
    )
    copies[0].wait()
    copies[1].wait()
    size = jnp.exp2(-levels_in[...].astype(F32))
    in_use = jnp.where(lane_index(1) < live_ref[0], 1.0, 0.0).astype(F32)
    kinetic[...] = jnp.broadcast_to(size / 4.0 * in_use, (8, LANES))
    volume = size * size * size / 8.0 * in_use
    for j in ALL_ROWS:
        line = volume * float(QUADRATURE[j]) * coefficient[j : j + 1, :]
        coefficient[j : j + 1, :] = line


def apply_cells(values, terms, kinetic, coefficient, rows, vectors):
    def one(t, carry):
        part = pl.ds(pl.multiple_of(8 * t, 8), 8)
        for j in rows:
            total = None
            for k in np.flatnonzero(STIFFNESS[j]):
                term = values[int(k), part, :] * float(STIFFNESS[j, k])
                total = term if total is None else total + term
            weight = jnp.broadcast_to(coefficient[j : j + 1, :], (8, LANES))
            terms.store(j, kinetic[...] * total + weight * values[j, part, :], part)
        return carry

    lax.fori_loop(0, vectors // 8, one, 0)


def join_layer(terms, layers, vectors):
    lane = lane_index(8)
    moves = [below_of(lane, axis) + above_of(lane, axis) for axis in range(2)]

    def one(t, carry):
        part = pl.ds(pl.multiple_of(8 * t, 8), 8)
        for axis in range(2):
            before, has_before, after, has_after = moves[axis]
            for other in range(5):
                for c in layers:
                    start = node(0, other, c) if axis == 0 else node(other, 0, c)
                    end = node(4, other, c) if axis == 0 else node(other, 4, c)
                    first, last = terms.load(start, part), terms.load(end, part)
                    joined = first + jnp.where(has_before, pick(last, before), 0.0)
                    terms.store(start, joined, part)
                    terms.store(end, jnp.where(has_after, pick(joined, after), last), part)
        return carry

    lax.fori_loop(0, vectors // 8, one, 0)


def pack_lower(low, face_out, vectors):
    upper = upper_lanes(vectors)
    for i in range(13):
        second = min(2 * i + 1, 24)
        face_out[i] = jnp.where(upper, up_layer(low[second]), low[2 * i]).astype(BF16)


def pack_upper(top, face_out, vectors):
    upper = upper_lanes(vectors)
    for i in range(13):
        second = min(2 * i + 1, 24)
        face_out[i] = jnp.where(upper, top[2 * i], down_layer(top[second])).astype(BF16)


def from_below(packed, ab):
    return packed if ab % 2 == 1 else down_layer(packed)


def from_above(packed, ab):
    return packed if ab % 2 == 1 else up_layer(packed)


def first_faces_kernel(
    vectors, wave_mid, wave_top, mass_mid, mass_top, ghost, kinetic, coefficient,
    values, wave_low, mass_low, low, top, face_down, face_up,
):
    upper, upper_one = upper_lanes(vectors), upper_lanes(1)
    for ab in range(25):
        packed = ghost[ab // 2]
        wave_low[ab] = jnp.where(upper, up_layer(wave_top[ab]), from_below(packed[0:vectors], ab))
        mass_low[ab : ab + 1, :] = jnp.where(
            upper_one,
            up_layer(mass_top[ab : ab + 1, :]),
            from_below(packed[vectors : vectors + 1], ab),
        )
    wave, mass = Nodes(wave_low, wave_mid, wave_top), Nodes(mass_low, mass_mid, mass_top)
    for j in ALL_ROWS:
        values[j] = (wave.load(j) * mass.line(j)).astype(BF16).astype(F32)
    terms = Nodes(low, None, top)
    apply_cells(values, terms, kinetic, coefficient, LOW_ROWS + TOP_ROWS, vectors)
    join_layer(terms, (0, 4), vectors)
    pack_lower(low, face_down, vectors)
    pack_upper(top, face_up, vectors)


def rest_kernel(vectors, values, kinetic, coefficient, mid):
    terms = Nodes(None, mid, None)
    apply_cells(values, terms, kinetic, coefficient, MID_ROWS, vectors)
    join_layer(terms, (1, 2, 3), vectors)


def second_faces_kernel(
    vectors, low, mid, top, wave_low, wave_mid, wave_top, mass_low, mass_mid, mass_top,
    above, below, kinetic, coefficient, center_ref, halfwidth_ref,
    values, base_mid, base_top, low_out, face_down,
):
    upper = upper_lanes(vectors)
    center = center_ref[0]
    inverse = 1.0 / jnp.full((1, LANES), halfwidth_ref[0], F32)
    again = (-2.0 * center) * inverse
    sums = Nodes(low, mid, top)
    wave, mass = Nodes(wave_low, wave_mid, wave_top), Nodes(mass_low, mass_mid, mass_top)
    base = Nodes(None, base_mid, base_top)

    def degree_one(j, total):
        one = (mass.line(j) * total - center * wave.load(j)) * inverse
        values[j] = (one * mass.line(j)).astype(BF16).astype(F32)
        if j % 5 > 0:
            base.store(j, again * one - wave.load(j))

    for ab in range(25):
        first, last = low[ab], top[ab]
        shared = first + up_layer(last)
        incoming = from_below(below[ab // 2].astype(F32), ab)
        degree_one(5 * ab, jnp.where(upper, shared, first + incoming))
        incoming = from_above(above[ab // 2].astype(F32), ab)
        degree_one(5 * ab + 4, jnp.where(upper, last + incoming, down_layer(shared)))
        for c in range(1, 4):
            degree_one(5 * ab + c, mid[3 * ab + c - 1])
    terms = Nodes(low_out, None, None)
    apply_cells(values, terms, kinetic, coefficient, LOW_ROWS, vectors)
    join_layer(terms, (0,), vectors)
    pack_lower(low_out, face_down, vectors)


def scatter_rows(vectors, groups, plan, slots_ref, load, total):
    for start, count in tile_groups(plan):
        width = count * LANES
        pieces = []
        for kind, rows in plan[start : start + count]:
            halves = []
            for half in range(vectors // 8):
                part = slice(8 * half, 8 * (half + 1))
                halves.append(pack_tile(kind, rows, lambda j: load(j, part), jnp.float32(0)))
            pieces.append(jnp.concatenate(halves, 0).astype(BF16))
        value = jnp.concatenate(pieces, 1)
        slots = []
        for i in range(count):
            slot = slots_ref[start + i : start + i + 1, :]
            for place in repeated_places(*plan[start + i]):
                lane = lane_index(1)
                again = jnp.logical_and(axis_place(lane, 0) == place, axis_place(lane, 1) < 7)
                slot = jnp.where(again, 65535, slot)
            slots.append(slot)
        slot = jnp.concatenate(slots, 1)
        group = slot >> 8
        wide = jnp.broadcast_to(group.astype(F32).astype(BF16), (vectors, width))
        spread = [jnp.where(wide == BF16(h), value, BF16(0)) for h in range(groups)]
        spare = total.shape[0] - vectors * groups
        group_row = lax.broadcasted_iota(I32, (spare, width), 0)
        held = jnp.where(group_row == jnp.broadcast_to(group, (spare, width)), 1.0, 0.0)
        spread.append(held.astype(BF16))
        moved = lax.dot_general(
            jnp.concatenate(spread, 0),
            one_hot(slot, width),
            (((1,), (1,)), ((), ())),
            preferred_element_type=F32,
        )
        if start == 0:
            total[...] = moved
        else:
            total[...] += moved


def second_rest_kernel(
    vectors, values, kinetic, coefficient, low, mass_mid, mass_top, base_mid, base_top, slots,
    wave_hbm, earlier_hbm, center_ref, halfwidth_ref,
    total, done_top, alone, *rest,
):
    earlier, (mid, top, wave_in, sems) = rest[:-4], rest[-4:]
    copy = pltpu.make_async_copy(wave_hbm, wave_in, sems.at[0])
    copy.start()
    loads = []
    for i, part in enumerate(earlier):
        size = part.shape[0]
        source = earlier_hbm.at[size * i : size * (i + 1), :]
        loads.append(pltpu.make_async_copy(source, part, sems.at[1 + i]))
        loads[-1].start()
    groups = wave_in.shape[1] // 256
    center = center_ref[0]
    inverse = 1.0 / jnp.full((1, LANES), halfwidth_ref[0], F32)
    terms = Nodes(None, mid, top)
    apply_cells(values, terms, kinetic, coefficient, MID_ROWS + TOP_ROWS, vectors)
    join_layer(terms, (1, 2, 3, 4), vectors)
    upper = upper_lanes(vectors)
    for ab in range(25):
        last = top[ab]
        joined = jnp.where(upper, last, down_layer(low[ab]) + last)
        line = (2.0 * inverse) * mass_top[ab : ab + 1, :]
        done_top[ab] = base_top[ab] + line * joined

    def load(j, part):
        row = mid_row(j)
        line = (2.0 * inverse) * mass_mid[row : row + 1, :]
        return base_mid[row, part, :] + line * mid[row, part, :]

    scatter_rows(vectors, groups, MID_PLAN, slots, load, total)
    copy.wait()
    wide_inverse = jnp.concatenate([inverse, inverse], 1)
    for h in range(groups):
        wave = wave_in[:, 256 * h : 256 * (h + 1)]
        one = -center * wave * wide_inverse
        alone[:, 256 * h : 256 * (h + 1)] = (
            (-2.0 * center) * wide_inverse * one - wave
        ).astype(BF16)
    for load in loads:
        load.wait()


def scatter_top_kernel(
    vectors, slots, before, done_top, mass_top, above, alone, halfwidth_ref, *rest
):
    outs, (placed, total) = rest[:-2], rest[-2:]
    groups = alone.shape[1] // 256
    base = vectors * groups
    upper = upper_lanes(8)
    inverse = 1.0 / jnp.full((1, LANES), halfwidth_ref[0], F32)

    def load(j, part):
        ab = j // 5
        incoming = from_above(above[ab // 2].astype(F32)[part], ab)
        share = (2.0 * inverse) * mass_top[ab : ab + 1, :] * incoming
        return done_top[ab, part, :] + jnp.where(upper, share, 0.0)

    scatter_rows(vectors, groups, TOP_PLAN, slots, load, total)
    parts, part = len(outs), lax.axis_index("vecs")
    quarter = groups // parts
    for h in range(groups):
        rows = slice(vectors * h, vectors * (h + 1))
        count = total[base + h : base + h + 1, :] + before[base + h : base + h + 1, :]
        value = total[rows, :] + before[rows, :]
        own = alone[:, 256 * h : 256 * (h + 1)].astype(F32)
        at = h % quarter
        away = lax.rem(h // quarter + parts - part, parts)
        placed[away, :, 256 * at : 256 * (at + 1)] = jnp.where(count > 0.5, value, own).astype(BF16)
    for away, out in enumerate(outs):
        out[...] = placed[away]


def earlier_rows(earlier, start, size, columns=slice(None)):
    pieces, height = [], earlier[0].shape[0]
    while size > 0:
        block, at = divmod(start, height)
        count = min(size, height - at)
        pieces.append(earlier[block][at : at + count, columns])
        start, size = start + count, size - count
    return pieces


def project_kernel(cores, parts, share, other, quarter, *rest):
    earlier, (out,) = rest[:-1], rest[-1:]
    half, block = share // 2, parts * share
    total = sum(part.shape[0] for part in earlier)
    here = lax.rem(lax.axis_index("cells"), cores)
    for core in range(cores):

        @pl.when(here == (1 - core if other else core))
        def _():
            pieces = []
            for start in range(core * block, total, cores * block):
                pieces += earlier_rows(earlier, start, block)
            product = lax.dot_general(
                jnp.concatenate(pieces, 0),
                quarter[...],
                (((1,), (1,)), ((), ())),
                preferred_element_type=F32,
            )
            product = product.reshape(out.shape[0], share, product.shape[-1])
            out[...] = jnp.concatenate([product[:, :half], product[:, half:]], 2)


def gather_pieces_kernel(parts, *refs):
    quarter = refs[-1]
    for away, piece in enumerate(refs[:-1]):
        size = piece.shape[0]
        source = lax.rem(lax.axis_index("vecs") + parts - away, parts)
        quarter[pl.ds(pl.multiple_of(size * source, size), size), :] = piece[...]


def pair_sum_kernel(keep, received, out):
    out[...] = (keep[...] + received[...]).astype(out.dtype)


def own_rows_kernel(shares, own_rows, spread):
    own = jnp.sum(shares[...].astype(F32), 0)
    columns = own.shape[1] // 2
    own_rows[...] = jnp.concatenate([own[:, :columns], own[:, columns:]], 0)
    spread[...] = jnp.broadcast_to(own[None], spread.shape).astype(BF16)


def filter_kernel(cores, parts, share, other, spread, before, *rest):
    earlier, (out, low) = rest[:-2], rest[-2:]
    half, block = share // 2, parts * share
    columns = spread.shape[-1] // 2
    total = sum(part.shape[0] for part in earlier)
    value = spread[...].astype(F32)
    value = jnp.concatenate([value[:, :, :columns], value[:, :, columns:]], 1)
    low[...] = value.reshape(low.shape).astype(BF16)
    here = lax.rem(lax.axis_index("cells"), cores)
    width = 256
    for core in range(cores):

        @pl.when(here == (1 - core if other else core))
        def _():
            for i in range(out.shape[1] // width):
                at = slice(width * i, width * (i + 1))
                pieces = []
                for start in range(core * block, total, cores * block):
                    pieces += earlier_rows(earlier, start, block, at)
                product = lax.dot_general(
                    low[...],
                    jnp.concatenate(pieces, 0),
                    (((0,), (0,)), ((), ())),
                    preferred_element_type=F32,
                )
                out[:, at] = before[:, at].astype(F32) - product


VMEM_SPEC = pl.BlockSpec(memory_space=pltpu.VMEM)
SMEM_SPEC = pl.BlockSpec(memory_space=pltpu.SMEM)
HBM_SPEC = pl.BlockSpec(memory_space=pltpu.HBM)


def call(kernel, name, out_shape, specs, scratch, *operands):
    return pl.pallas_call(
        kernel,
        out_shape=out_shape,
        in_specs=[{"v": VMEM_SPEC, "s": SMEM_SPEC, "h": HBM_SPEC}[letter] for letter in specs],
        out_specs=jax.tree.map(lambda _: VMEM_SPEC, out_shape),
        scratch_shapes=scratch,
        compiler_params=pltpu.CompilerParams(vmem_limit_bytes=VMEM_LIMIT),
        name=name,
    )(*[
        pltpu.with_memory_space_constraint(operand, pltpu.HBM) if letter == "h" else operand
        for letter, operand in zip(specs, operands)
    ])


def passed_along(value, axis, steps):
    count = lax.axis_size(axis)
    leading, last = (max(0, -steps), min(count, count - steps))
    return lax.ppermute(value, axis, [(source, source + steps) for source in range(leading, last)])


def per_device(
    wave_block, connectivity, send_list, levels, live_cells, potential, mass_scale,
    center, halfwidth, earlier_vectors,
):
    vectors, owned = wave_block.shape
    groups = owned // 256
    table_rows = vectors * groups + 48
    cells, parts = lax.axis_size("cells"), lax.axis_size("vecs")
    devices, cores = cells * parts, 2
    turn = lambda away: [(i, (i + away) % parts) for i in range(parts)]
    center, halfwidth = center.reshape(1), halfwidth.reshape(1)

    def shape(*sizes, kind=F32):
        return jax.ShapeDtypeStruct(sizes, kind)

    def rows(count):
        return shape(count, vectors, LANES)

    def lines(count):
        return shape(count, LANES)

    packed = shape(13, vectors, LANES, kind=BF16)
    scratch_rows = lambda count: pltpu.VMEM((count, vectors, LANES), F32)
    wave_scratch = pltpu.VMEM((vectors, owned), F32)

    extra = lambda count: [scratch_rows(count), pltpu.VMEM((count, 8, LANES), F32)]
    table, conn, slots_top, wave_top, mass_top, face = call(
        lambda *refs: gather_face_kernel(vectors, *refs),
        "gather_face",
        (
            shape(table_rows, 512, kind=BF16), shape(125, LANES, kind=I32),
            shape(len(TOP_PLAN), LANES, kind=I32), rows(25), lines(25),
            shape(13, vectors + 8, LANES),
        ),
        "hhh",
        [wave_scratch, pltpu.VMEM((owned // LANES, LANES), F32), *extra(2), pltpu.SemaphoreType.DMA((3,))],
        connectivity, wave_block, mass_scale.reshape(owned // LANES, LANES),
    )
    ghost = passed_along(face, "cells", 1)
    slots_mid, wave_mid, mass_mid, kinetic, coefficient = call(
        lambda *refs: gather_rest_kernel(vectors, groups, *refs),
        "gather_rest",
        (
            shape(len(MID_PLAN), LANES, kind=I32), rows(75), lines(75), lines(8), lines(125),
        ),
        "vvhhs",
        [pltpu.VMEM((1, LANES), I32), *extra(4), pltpu.SemaphoreType.DMA((2,))],
        table, conn, potential, levels.reshape(1, LANES), live_cells,
    )
    values, wave_low, mass_low, low, top, face_down, face_up = call(
        lambda *refs: first_faces_kernel(vectors, *refs),
        "first_faces",
        (rows(125), rows(25), lines(25), rows(25), rows(25), packed, packed),
        "vvvvvvv",
        [],
        wave_mid, wave_top, mass_mid, mass_top, ghost, kinetic, coefficient,
    )
    above = passed_along(face_down, "cells", -1)
    below = passed_along(face_up, "cells", 1)
    mid = call(
        lambda *refs: rest_kernel(vectors, *refs), "first_rest", rows(75), "vvv", [],
        values, kinetic, coefficient,
    )
    values, base_mid, base_top, low, face_down = call(
        lambda *refs: second_faces_kernel(vectors, *refs),
        "second_faces",
        (rows(125), rows(75), rows(25), rows(25), packed),
        "v" * 13 + "ss",
        [],
        low, mid, top, wave_low, wave_mid, wave_top, mass_low, mass_mid, mass_top,
        above, below, kinetic, coefficient, center, halfwidth,
    )
    above = passed_along(face_down, "cells", -1)
    before, done_top, alone, *earlier = call(
        lambda *refs: second_rest_kernel(vectors, *refs),
        "second_rest",
        (
            shape(table_rows, 256), rows(25), shape(vectors, owned, kind=BF16),
            *[shape(earlier_vectors.shape[0] // BLOCKS, owned // parts, kind=BF16)] * BLOCKS,
        ),
        "v" * 9 + "hhss",
        [scratch_rows(75), scratch_rows(25), wave_scratch, pltpu.SemaphoreType.DMA((1 + BLOCKS,))],
        values, kinetic, coefficient, low, mass_mid, mass_top, base_mid, base_top, slots_mid,
        wave_block, earlier_vectors, center, halfwidth,
    )
    pieces = call(
        lambda *refs: scatter_top_kernel(vectors, *refs),
        "scatter_top",
        (shape(vectors, owned // parts, kind=BF16),) * parts,
        "vvvvvvs",
        [pltpu.VMEM((parts, vectors, owned // parts), BF16), pltpu.VMEM((table_rows, 256), F32)],
        slots_top, before, done_top, mass_top, above, alone, halfwidth,
    )
    pieces = [
        lax.ppermute(piece, "vecs", turn(away)) if away else piece
        for away, piece in enumerate(pieces)
    ]
    total_vectors = parts * vectors
    share = earlier_vectors.shape[0] // devices
    half, peers = share // 2, devices // cores
    pair = [(i, i ^ 1) for i in range(cells)]
    same_core = [
        [(cores * block + k) * parts + part for block in range(cells // cores) for part in range(parts)]
        for k in range(cores)
    ]
    sent = shape(peers, half, 2 * total_vectors)
    quarter = call(
        lambda *refs: gather_pieces_kernel(parts, *refs),
        "gather_pieces",
        shape(total_vectors, owned // parts, kind=BF16),
        "v" * parts, [], *pieces,
    )
    send, keep = [
        call(
            lambda *refs, other=other: project_kernel(cores, parts, share, other, *refs),
            "project_other" if other else "project_own",
            sent, "v" * (1 + BLOCKS), [], quarter, *earlier,
        )
        for other in (True, False)
    ]
    shares = call(
        pair_sum_kernel, "pair_sum", shape(*sent.shape, kind=BF16), "vv", [],
        keep, lax.ppermute(send, "cells", pair),
    )
    shares = lax.all_to_all(
        shares, AXES, split_axis=0, concat_axis=0, tiled=True, axis_index_groups=same_core
    )
    own_rows, mine = call(
        own_rows_kernel,
        "own_rows",
        (shape(share, total_vectors), shape(peers, half, 2 * total_vectors, kind=BF16)),
        "v", [], shares,
    )
    mine = lax.all_to_all(
        mine, AXES, split_axis=0, concat_axis=0, tiled=True, axis_index_groups=same_core
    )
    theirs = lax.ppermute(mine, "cells", pair)
    filtered = quarter
    for other, spread in ((False, mine), (True, theirs)):
        filtered = call(
            lambda *refs, other=other: filter_kernel(cores, parts, share, other, *refs),
            "filter_other" if other else "filter_own",
            shape(total_vectors, owned // parts),
            "vv" + "v" * BLOCKS,
            [pltpu.VMEM((peers * share, total_vectors), BF16)],
            spread, filtered, *earlier,
        )
    return (filtered, own_rows)


def solution(mesh):
    in_specs = (
        P("vecs", "cells"),
        P(None, "cells"),
        P("cells"),
        P("cells"),
        P("cells"),
        P(None, "cells"),
        P("cells"),
        P(),
        P(),
        P(None, AXES),
    )
    out_specs = (P(None, AXES), P(AXES, None))
    return jax.shard_map(
        per_device, mesh=mesh, in_specs=in_specs, out_specs=out_specs, check_vma=False
    )
```

```python
import math

import jax
import jax.numpy as jnp
import numpy as np
from jax import lax
from jax.experimental import pallas as pl
from jax.experimental.pallas import tpu as pltpu
from jax.sharding import PartitionSpec as P

F32, BF16, I32 = jnp.float32, jnp.bfloat16, jnp.int32
AXES = ("cells", "vecs")
LANES = 128
BLOCKS = 8
VMEM_LIMIT = 20 * 2**20


def gll_tables():
    root_value = math.sqrt(3.0 / 7.0)
    points = np.array([-1.0, -root_value, 0.0, root_value, 1.0])
    weights = np.array([0.1, 49.0 / 90.0, 32.0 / 45.0, 49.0 / 90.0, 0.1])
    barycentric = np.ones(5)
    for node_index in range(5):
        for other_node in range(5):
            if other_node != node_index:
                barycentric[node_index] = barycentric[node_index] / (
                    points[node_index] - points[other_node]
                )
    derivative = np.zeros((5, 5))
    for row_index in range(5):
        for col_index in range(5):
            if row_index != col_index:
                derivative[row_index, col_index] = (
                    barycentric[col_index]
                    / barycentric[row_index]
                    / (points[row_index] - points[col_index])
                )
        derivative[row_index, row_index] = -np.sum(derivative[row_index])
    mass_one = np.zeros((5, 5))
    for node_index in range(5):
        mass_one[node_index, node_index] = weights[node_index]
    laplace_one = derivative.T @ mass_one @ derivative
    stiffness = (
        np.kron(np.kron(laplace_one, mass_one), mass_one)
        + np.kron(np.kron(mass_one, laplace_one), mass_one)
        + np.kron(np.kron(mass_one, mass_one), laplace_one)
    )
    quadrature = np.kron(np.kron(weights, weights), weights)
    return (stiffness.astype(np.float32), quadrature.astype(np.float32))


STIFFNESS, QUADRATURE = gll_tables()
STIFFNESS = STIFFNESS.astype(jnp.bfloat16).astype(np.float32)


def node(a, b, c):
    return 25 * a + 5 * b + c


def lane_index(rows):
    return lax.broadcasted_iota(I32, (rows, LANES), 1)


def axis_bits(lane, axis):
    return [(lane >> bit) & 1 for bit in ((0, 3, 5), (1, 4, 6))[axis]]


def axis_place(lane, axis):
    low, mid, high = axis_bits(lane, axis)
    return low + 2 * mid + 4 * high


def below_of(lane, axis):
    low, mid, high = axis_bits(lane, axis)
    scale = 1 + axis
    step = jnp.where(low == 1, 1, jnp.where(mid == 1, 7, 23)) * scale
    first = axis_place(lane, axis) == 0
    return jnp.where(first, lane, lane - step), jnp.logical_not(first)


def above_of(lane, axis):
    low, mid, high = axis_bits(lane, axis)
    scale = 1 + axis
    step = jnp.where(low == 0, 1, jnp.where(mid == 0, 7, 23)) * scale
    last = axis_place(lane, axis) == 7
    return jnp.where(last, lane, lane + step), jnp.logical_not(last)


def pick(values, index):
    return jnp.take_along_axis(values, index, axis=1)


def up_layer(values):
    return pltpu.roll(values, 4, 1)


def down_layer(values):
    return pltpu.roll(values, LANES - 4, 1)


def split_low(values):
    high = values.astype(BF16)
    return high, (values - high.astype(F32)).astype(BF16)


class Nodes:
    def __init__(self, low, mid, top):
        self.low, self.mid, self.top = low, mid, top

    def at(self, j):
        ab, c = divmod(j, 5)
        if c == 0:
            return self.low, ab
        if c == 4:
            return self.top, ab
        return self.mid, 3 * ab + c - 1

    def load(self, j, part=slice(None)):
        ref, row = self.at(j)
        return ref[row, part, :]

    def store(self, j, value, part=slice(None)):
        ref, row = self.at(j)
        ref[row, part, :] = value

    def line(self, j):
        ref, row = self.at(j)
        return ref[row : row + 1, :]

    def store_line(self, j, value):
        ref, row = self.at(j)
        ref[row : row + 1, :] = value


ALL_ROWS = list(range(125))
MID_ROWS = [j for j in ALL_ROWS if j % 5 in (1, 2, 3)]
LOW_ROWS = [j for j in ALL_ROWS if j % 5 == 0]
TOP_ROWS = [j for j in ALL_ROWS if j % 5 == 4]


def upper_lanes(rows):
    return (lane_index(rows) >> 2) & 1 == 1


def one_hot(slots, width):
    place = lax.broadcasted_iota(I32, (256, width), 0).astype(F32).astype(BF16)
    within = jnp.broadcast_to((slots & 255).astype(F32).astype(BF16), (256, width))
    return jnp.where(place == within, BF16(1), BF16(0))


AXIS_MASK = (1 + 8 + 32, 2 + 16 + 64)


def place_bits(place, axis):
    return [(place & 1) + (place & 2) * 4 + (place & 4) * 8, (place & 1) * 2 + (place & 2) * 8 + (place & 4) * 16][axis]


def tile_plan(layers):
    tiles = [("all", [node(a, b, c)]) for a in range(4) for b in range(4) for c in layers]
    for axis in range(2):
        rows = [
            node(4, k, c) if axis == 0 else node(k, 4, c)
            for k in range(5 - axis)
            for c in layers
        ]
        tiles += [(axis, rows[i : i + 8]) for i in range(0, len(rows), 8)]
    return tiles


MID_PLAN, TOP_PLAN = tile_plan((1, 2, 3)), tile_plan((4,))


def tile_groups(plan):
    count = len(plan)
    fives = count % 4
    sizes = [5] * fives + [4] * ((count - 5 * fives) // 4)
    starts = np.cumsum([0] + sizes)
    return [(int(start), size) for start, size in zip(starts, sizes)]


def pack_tile(kind, rows, load, empty):
    if kind == "all":
        return load(rows[0])
    lane = lane_index(8)
    place, last = axis_place(lane, kind), lane | AXIS_MASK[kind]
    tile = jnp.full((8, LANES), empty)
    for i, j in enumerate(rows):
        tile = jnp.where(place == i, pick(load(j), last), tile)
    return tile


def repeated_places(kind, rows):
    return [i for i, j in enumerate(rows) if kind == 0 and j // 5 == 24]


def pack_slots(plan, conn, slots):
    def load(j):
        return jnp.broadcast_to(conn[j : j + 1, :], (8, LANES))

    for i, (kind, rows) in enumerate(plan):
        tile = pack_tile(kind, rows, load, jnp.int32(65535))
        slots[i : i + 1, :] = tile[0:1, :]


def unpack_tiles(plan, extra, load, store):
    lane = lane_index(8)
    for axis in (1, 0):
        after, has_after = above_of(lane, axis)
        for i, (kind, rows) in enumerate(plan):
            if kind != axis:
                continue
            tile = extra(i)
            for place, j in enumerate(rows):
                source = (lane & ~AXIS_MASK[axis]) | place_bits(place, axis)
                inner = pick(load(j - (100 if axis == 0 else 20)), after)
                store(j, jnp.where(has_after, inner, pick(tile, source)))


def gather_rows(vectors, groups, plan, row_of, slots_ref, table, wave, mass, wave_extra, mass_extra):
    base = vectors * groups
    whole = sum(kind == "all" for kind, _ in plan)
    for start, count in tile_groups(plan):
        width = count * LANES
        slots = jnp.concatenate([slots_ref[start + i : start + i + 1, :] for i in range(count)], 1)
        chosen = one_hot(slots, width)
        found = jnp.dot(
            table[...], jnp.concatenate([chosen, chosen], 0), preferred_element_type=F32
        )
        group = slots >> 8
        wide = jnp.broadcast_to(group, (vectors, width))
        total = jnp.zeros((vectors, width), F32)
        for h in range(groups):
            total = jnp.where(wide == h, found[vectors * h : vectors * (h + 1)], total)
        group_row = lax.broadcasted_iota(I32, (groups, width), 0)
        mine = group_row == jnp.broadcast_to(group, (groups, width))
        line = jnp.sum(jnp.where(mine, found[base : base + groups], 0.0), 0, keepdims=True)
        for i in range(count):
            kind, rows = plan[start + i]
            columns = slice(LANES * i, LANES * (i + 1))
            if kind == "all":
                row = row_of(rows[0])
                wave[row] = total[:, columns]
                mass[row : row + 1, :] = line[:, columns]
            else:
                wave_extra[start + i - whole] = total[:, columns]
                mass_extra[start + i - whole] = jnp.broadcast_to(line[:, columns], (8, LANES))
    for half in range(vectors // 8):
        part = slice(8 * half, 8 * (half + 1))

        def store(j, value):
            wave[row_of(j), part, :] = value

        unpack_tiles(
            plan, lambda i: wave_extra[i - whole, part, :], lambda j: wave[row_of(j), part, :], store
        )

    def store_line(j, value):
        mass[row_of(j) : row_of(j) + 1, :] = value[0:1, :]

    def load_line(j):
        return jnp.broadcast_to(mass[row_of(j) : row_of(j) + 1, :], (8, LANES))

    unpack_tiles(plan, lambda i: mass_extra[i - whole], load_line, store_line)


def mid_row(j):
    return 3 * (j // 5) + j % 5 - 1


def top_row(j):
    return j // 5


def gather_face_kernel(
    vectors, conn_hbm, wave_hbm, mass_hbm, table, conn, slots, wave_top, mass_top, face_out,
    wave_in, mass_in, wave_extra, mass_extra, sems,
):
    copies = [
        pltpu.make_async_copy(conn_hbm, conn, sems.at[2]),
        pltpu.make_async_copy(wave_hbm, wave_in, sems.at[0]),
        pltpu.make_async_copy(mass_hbm, mass_in, sems.at[1]),
    ]
    for copy in copies:
        copy.start()
    copies[0].wait()
    pack_slots(TOP_PLAN, conn, slots)
    for copy in copies[1:]:
        copy.wait()
    groups = wave_in.shape[1] // 256
    base = vectors * groups
    high, low = split_low(wave_in[...])
    for h in range(groups):
        table[vectors * h : vectors * (h + 1), 0:256] = high[:, 256 * h : 256 * (h + 1)]
        table[vectors * h : vectors * (h + 1), 256:512] = low[:, 256 * h : 256 * (h + 1)]
    for half in range(2):
        high, low = split_low(mass_in[pl.ds(half, groups, stride=2), :])
        spare = jnp.zeros((table.shape[0] - base - groups, LANES), F32)
        columns = slice(LANES * half, LANES * (half + 1))
        table[base:, columns] = jnp.concatenate([high.astype(F32), spare], 0).astype(BF16)
        columns = slice(256 + LANES * half, 256 + LANES * (half + 1))
        table[base:, columns] = jnp.concatenate([low.astype(F32), spare], 0).astype(BF16)
    gather_rows(
        vectors, groups, TOP_PLAN, top_row, slots, table, wave_top, mass_top, wave_extra, mass_extra
    )
    upper, upper_one = upper_lanes(vectors), upper_lanes(1)
    for i in range(13):
        second = min(2 * i + 1, 24)
        face_out[i, 0:vectors, :] = jnp.where(upper, wave_top[2 * i], down_layer(wave_top[second]))
        packed = jnp.where(
            upper_one,
            mass_top[2 * i : 2 * i + 1, :],
            down_layer(mass_top[second : second + 1, :]),
        )
        face_out[i, vectors : vectors + 8, :] = jnp.broadcast_to(packed, (8, LANES))


def gather_rest_kernel(
    vectors, groups, table, conn, potential_hbm, levels_hbm, live_ref,
    slots, wave_mid, mass_mid, kinetic, coefficient, levels_in, wave_extra, mass_extra, sems,
):
    copies = [
        pltpu.make_async_copy(potential_hbm, coefficient, sems.at[0]),
        pltpu.make_async_copy(levels_hbm, levels_in, sems.at[1]),
    ]
    for copy in copies:
        copy.start()
    pack_slots(MID_PLAN, conn, slots)
    gather_rows(
        vectors, groups, MID_PLAN, mid_row, slots, table, wave_mid, mass_mid, wave_extra, mass_extra
    )
    copies[0].wait()
    copies[1].wait()
    size = jnp.exp2(-levels_in[...].astype(F32))
    in_use = jnp.where(lane_index(1) < live_ref[0], 1.0, 0.0).astype(F32)
    kinetic[...] = jnp.broadcast_to(size / 4.0 * in_use, (8, LANES))
    volume = size * size * size / 8.0 * in_use
    for j in ALL_ROWS:
        line = volume * float(QUADRATURE[j]) * coefficient[j : j + 1, :]
        coefficient[j : j + 1, :] = line


def apply_cells(values, terms, kinetic, coefficient, rows, vectors):
    def one(t, carry):
        part = pl.ds(pl.multiple_of(8 * t, 8), 8)
        for j in rows:
            total = None
            for k in np.flatnonzero(STIFFNESS[j]):
                term = values[int(k), part, :] * float(STIFFNESS[j, k])
                total = term if total is None else total + term
            weight = jnp.broadcast_to(coefficient[j : j + 1, :], (8, LANES))
            terms.store(j, kinetic[...] * total + weight * values[j, part, :], part)
        return carry

    lax.fori_loop(0, vectors // 8, one, 0)


def join_layer(terms, layers, vectors):
    lane = lane_index(8)
    moves = [below_of(lane, axis) + above_of(lane, axis) for axis in range(2)]

    def one(t, carry):
        part = pl.ds(pl.multiple_of(8 * t, 8), 8)
        for axis in range(2):
            before, has_before, after, has_after = moves[axis]
            for other in range(5):
                for c in layers:
                    start = node(0, other, c) if axis == 0 else node(other, 0, c)
                    end = node(4, other, c) if axis == 0 else node(other, 4, c)
                    first, last = terms.load(start, part), terms.load(end, part)
                    joined = first + jnp.where(has_before, pick(last, before), 0.0)
                    terms.store(start, joined, part)
                    terms.store(end, jnp.where(has_after, pick(joined, after), last), part)
        return carry

    lax.fori_loop(0, vectors // 8, one, 0)


def pack_lower(low, face_out, vectors):
    upper = upper_lanes(vectors)
    for i in range(13):
        second = min(2 * i + 1, 24)
        face_out[i] = jnp.where(upper, up_layer(low[second]), low[2 * i]).astype(BF16)


def pack_upper(top, face_out, vectors):
    upper = upper_lanes(vectors)
    for i in range(13):
        second = min(2 * i + 1, 24)
        face_out[i] = jnp.where(upper, top[2 * i], down_layer(top[second])).astype(BF16)


def from_below(packed, ab):
    return packed if ab % 2 == 1 else down_layer(packed)


def from_above(packed, ab):
    return packed if ab % 2 == 1 else up_layer(packed)


def first_faces_kernel(
    vectors, wave_mid, wave_top, mass_mid, mass_top, ghost, kinetic, coefficient,
    values, wave_low, mass_low, low, top, face_down, face_up,
):
    upper, upper_one = upper_lanes(vectors), upper_lanes(1)
    for ab in range(25):
        packed = ghost[ab // 2]
        wave_low[ab] = jnp.where(upper, up_layer(wave_top[ab]), from_below(packed[0:vectors], ab))
        mass_low[ab : ab + 1, :] = jnp.where(
            upper_one,
            up_layer(mass_top[ab : ab + 1, :]),
            from_below(packed[vectors : vectors + 1], ab),
        )
    wave, mass = Nodes(wave_low, wave_mid, wave_top), Nodes(mass_low, mass_mid, mass_top)
    for j in ALL_ROWS:
        values[j] = (wave.load(j) * mass.line(j)).astype(BF16).astype(F32)
    terms = Nodes(low, None, top)
    apply_cells(values, terms, kinetic, coefficient, LOW_ROWS + TOP_ROWS, vectors)
    join_layer(terms, (0, 4), vectors)
    pack_lower(low, face_down, vectors)
    pack_upper(top, face_up, vectors)


def rest_kernel(vectors, values, kinetic, coefficient, mid):
    terms = Nodes(None, mid, None)
    apply_cells(values, terms, kinetic, coefficient, MID_ROWS, vectors)
    join_layer(terms, (1, 2, 3), vectors)


def second_faces_kernel(
    vectors, low, mid, top, wave_low, wave_mid, wave_top, mass_low, mass_mid, mass_top,
    above, below, kinetic, coefficient, center_ref, halfwidth_ref,
    values, base_mid, base_top, low_out, face_down,
):
    upper = upper_lanes(vectors)
    center = center_ref[0]
    inverse = 1.0 / jnp.full((1, LANES), halfwidth_ref[0], F32)
    again = (-2.0 * center) * inverse
    sums = Nodes(low, mid, top)
    wave, mass = Nodes(wave_low, wave_mid, wave_top), Nodes(mass_low, mass_mid, mass_top)
    base = Nodes(None, base_mid, base_top)

    def degree_one(j, total):
        one = (mass.line(j) * total - center * wave.load(j)) * inverse
        values[j] = (one * mass.line(j)).astype(BF16).astype(F32)
        if j % 5 > 0:
            base.store(j, again * one - wave.load(j))

    for ab in range(25):
        first, last = low[ab], top[ab]
        shared = first + up_layer(last)
        incoming = from_below(below[ab // 2].astype(F32), ab)
        degree_one(5 * ab, jnp.where(upper, shared, first + incoming))
        incoming = from_above(above[ab // 2].astype(F32), ab)
        degree_one(5 * ab + 4, jnp.where(upper, last + incoming, down_layer(shared)))
        for c in range(1, 4):
            degree_one(5 * ab + c, mid[3 * ab + c - 1])
    terms = Nodes(low_out, None, None)
    apply_cells(values, terms, kinetic, coefficient, LOW_ROWS, vectors)
    join_layer(terms, (0,), vectors)
    pack_lower(low_out, face_down, vectors)


def scatter_rows(vectors, groups, plan, slots_ref, load, total):
    for start, count in tile_groups(plan):
        width = count * LANES
        pieces = []
        for kind, rows in plan[start : start + count]:
            halves = []
            for half in range(vectors // 8):
                part = slice(8 * half, 8 * (half + 1))
                halves.append(pack_tile(kind, rows, lambda j: load(j, part), jnp.float32(0)))
            pieces.append(jnp.concatenate(halves, 0).astype(BF16))
        value = jnp.concatenate(pieces, 1)
        slots = []
        for i in range(count):
            slot = slots_ref[start + i : start + i + 1, :]
            for place in repeated_places(*plan[start + i]):
                lane = lane_index(1)
                again = jnp.logical_and(axis_place(lane, 0) == place, axis_place(lane, 1) < 7)
                slot = jnp.where(again, 65535, slot)
            slots.append(slot)
        slot = jnp.concatenate(slots, 1)
        group = slot >> 8
        wide = jnp.broadcast_to(group.astype(F32).astype(BF16), (vectors, width))
        spread = [jnp.where(wide == BF16(h), value, BF16(0)) for h in range(groups)]
        spare = total.shape[0] - vectors * groups
        group_row = lax.broadcasted_iota(I32, (spare, width), 0)
        held = jnp.where(group_row == jnp.broadcast_to(group, (spare, width)), 1.0, 0.0)
        spread.append(held.astype(BF16))
        moved = lax.dot_general(
            jnp.concatenate(spread, 0),
            one_hot(slot, width),
            (((1,), (1,)), ((), ())),
            preferred_element_type=F32,
        )
        if start == 0:
            total[...] = moved
        else:
            total[...] += moved


def second_rest_kernel(
    vectors, values, kinetic, coefficient, low, mass_mid, mass_top, base_mid, base_top, slots,
    wave_hbm, earlier_hbm, center_ref, halfwidth_ref,
    total, done_top, alone, *rest,
):
    earlier, (mid, top, wave_in, sems) = rest[:-4], rest[-4:]
    copy = pltpu.make_async_copy(wave_hbm, wave_in, sems.at[0])
    copy.start()
    loads = []
    for i, part in enumerate(earlier):
        size = part.shape[0]
        source = earlier_hbm.at[size * i : size * (i + 1), :]
        loads.append(pltpu.make_async_copy(source, part, sems.at[1 + i]))
        loads[-1].start()
    groups = wave_in.shape[1] // 256
    center = center_ref[0]
    inverse = 1.0 / jnp.full((1, LANES), halfwidth_ref[0], F32)
    terms = Nodes(None, mid, top)
    apply_cells(values, terms, kinetic, coefficient, MID_ROWS + TOP_ROWS, vectors)
    join_layer(terms, (1, 2, 3, 4), vectors)
    upper = upper_lanes(vectors)
    for ab in range(25):
        last = top[ab]
        joined = jnp.where(upper, last, down_layer(low[ab]) + last)
        line = (2.0 * inverse) * mass_top[ab : ab + 1, :]
        done_top[ab] = base_top[ab] + line * joined

    def load(j, part):
        row = mid_row(j)
        line = (2.0 * inverse) * mass_mid[row : row + 1, :]
        return base_mid[row, part, :] + line * mid[row, part, :]

    scatter_rows(vectors, groups, MID_PLAN, slots, load, total)
    copy.wait()
    wide_inverse = jnp.concatenate([inverse, inverse], 1)
    for h in range(groups):
        wave = wave_in[:, 256 * h : 256 * (h + 1)]
        one = -center * wave * wide_inverse
        alone[:, 256 * h : 256 * (h + 1)] = (
            (-2.0 * center) * wide_inverse * one - wave
        ).astype(BF16)
    for load in loads:
        load.wait()


def scatter_top_kernel(
    vectors, slots, before, done_top, mass_top, above, alone, halfwidth_ref, *rest
):
    outs, (placed, total) = rest[:-2], rest[-2:]
    groups = alone.shape[1] // 256
    base = vectors * groups
    upper = upper_lanes(8)
    inverse = 1.0 / jnp.full((1, LANES), halfwidth_ref[0], F32)

    def load(j, part):
        ab = j // 5
        incoming = from_above(above[ab // 2].astype(F32)[part], ab)
        share = (2.0 * inverse) * mass_top[ab : ab + 1, :] * incoming
        return done_top[ab, part, :] + jnp.where(upper, share, 0.0)

    scatter_rows(vectors, groups, TOP_PLAN, slots, load, total)
    parts, part = len(outs), lax.axis_index("vecs")
    quarter = groups // parts
    for h in range(groups):
        rows = slice(vectors * h, vectors * (h + 1))
        count = total[base + h : base + h + 1, :] + before[base + h : base + h + 1, :]
        value = total[rows, :] + before[rows, :]
        own = alone[:, 256 * h : 256 * (h + 1)].astype(F32)
        at = h % quarter
        away = lax.rem(h // quarter + parts - part, parts)
        placed[away, :, 256 * at : 256 * (at + 1)] = jnp.where(count > 0.5, value, own).astype(BF16)
    for away, out in enumerate(outs):
        out[...] = placed[away]


def earlier_rows(earlier, start, size, columns=slice(None)):
    pieces, height = [], earlier[0].shape[0]
    while size > 0:
        block, at = divmod(start, height)
        count = min(size, height - at)
        pieces.append(earlier[block][at : at + count, columns])
        start, size = start + count, size - count
    return pieces


def project_kernel(cores, parts, share, other, quarter, *rest):
    earlier, (out,) = rest[:-1], rest[-1:]
    half, block = share // 2, parts * share
    total = sum(part.shape[0] for part in earlier)
    here = lax.rem(lax.axis_index("cells"), cores)
    for core in range(cores):

        @pl.when(here == (1 - core if other else core))
        def _():
            pieces = []
            for start in range(core * block, total, cores * block):
                pieces += earlier_rows(earlier, start, block)
            product = lax.dot_general(
                jnp.concatenate(pieces, 0),
                quarter[...],
                (((1,), (1,)), ((), ())),
                preferred_element_type=F32,
            )
            product = product.reshape(out.shape[0], share, product.shape[-1])
            out[...] = jnp.concatenate([product[:, :half], product[:, half:]], 2)


def gather_pieces_kernel(parts, *refs):
    quarter = refs[-1]
    for away, piece in enumerate(refs[:-1]):
        size = piece.shape[0]
        source = lax.rem(lax.axis_index("vecs") + parts - away, parts)
        quarter[pl.ds(pl.multiple_of(size * source, size), size), :] = piece[...]


def pair_sum_kernel(keep, received, out):
    out[...] = (keep[...] + received[...]).astype(out.dtype)


def own_rows_kernel(shares, own_rows, spread):
    own = jnp.sum(shares[...].astype(F32), 0)
    columns = own.shape[1] // 2
    own_rows[...] = jnp.concatenate([own[:, :columns], own[:, columns:]], 0)
    spread[...] = jnp.broadcast_to(own.astype(BF16)[None], spread.shape)


def filter_kernel(cores, parts, share, other, spread, before, *rest):
    earlier, (out, low) = rest[:-2], rest[-2:]
    half, block = share // 2, parts * share
    columns = spread.shape[-1] // 2
    total = sum(part.shape[0] for part in earlier)
    value = spread[...].astype(F32)
    value = jnp.concatenate([value[:, :, :columns], value[:, :, columns:]], 1)
    low[...] = value.reshape(low.shape).astype(BF16)
    here = lax.rem(lax.axis_index("cells"), cores)
    width = 256
    for core in range(cores):

        @pl.when(here == (1 - core if other else core))
        def _():
            for i in range(out.shape[1] // width):
                at = slice(width * i, width * (i + 1))
                pieces = []
                for start in range(core * block, total, cores * block):
                    pieces += earlier_rows(earlier, start, block, at)
                product = lax.dot_general(
                    low[...],
                    jnp.concatenate(pieces, 0),
                    (((0,), (0,)), ((), ())),
                    preferred_element_type=F32,
                )
                out[:, at] = before[:, at].astype(F32) - product


VMEM_SPEC = pl.BlockSpec(memory_space=pltpu.VMEM)
SMEM_SPEC = pl.BlockSpec(memory_space=pltpu.SMEM)
HBM_SPEC = pl.BlockSpec(memory_space=pltpu.HBM)


def call(kernel, name, out_shape, specs, scratch, *operands):
    return pl.pallas_call(
        kernel,
        out_shape=out_shape,
        in_specs=[{"v": VMEM_SPEC, "s": SMEM_SPEC, "h": HBM_SPEC}[letter] for letter in specs],
        out_specs=jax.tree.map(lambda _: VMEM_SPEC, out_shape),
        scratch_shapes=scratch,
        compiler_params=pltpu.CompilerParams(vmem_limit_bytes=VMEM_LIMIT),
        name=name,
    )(*[
        pltpu.with_memory_space_constraint(operand, pltpu.HBM) if letter == "h" else operand
        for letter, operand in zip(specs, operands)
    ])


def passed_along(value, axis, steps):
    count = lax.axis_size(axis)
    leading, last = (max(0, -steps), min(count, count - steps))
    return lax.ppermute(value, axis, [(source, source + steps) for source in range(leading, last)])


def per_device(
    wave_block, connectivity, send_list, levels, live_cells, potential, mass_scale,
    center, halfwidth, earlier_vectors,
):
    vectors, owned = wave_block.shape
    groups = owned // 256
    table_rows = vectors * groups + 48
    cells, parts = lax.axis_size("cells"), lax.axis_size("vecs")
    devices, cores = cells * parts, 2
    turn = lambda away: [(i, (i + away) % parts) for i in range(parts)]
    center, halfwidth = center.reshape(1), halfwidth.reshape(1)

    def shape(*sizes, kind=F32):
        return jax.ShapeDtypeStruct(sizes, kind)

    def rows(count):
        return shape(count, vectors, LANES)

    def lines(count):
        return shape(count, LANES)

    packed = shape(13, vectors, LANES, kind=BF16)
    scratch_rows = lambda count: pltpu.VMEM((count, vectors, LANES), F32)
    wave_scratch = pltpu.VMEM((vectors, owned), F32)

    extra = lambda count: [scratch_rows(count), pltpu.VMEM((count, 8, LANES), F32)]
    table, conn, slots_top, wave_top, mass_top, face = call(
        lambda *refs: gather_face_kernel(vectors, *refs),
        "gather_face",
        (
            shape(table_rows, 512, kind=BF16), shape(125, LANES, kind=I32),
            shape(len(TOP_PLAN), LANES, kind=I32), rows(25), lines(25),
            shape(13, vectors + 8, LANES),
        ),
        "hhh",
        [wave_scratch, pltpu.VMEM((owned // LANES, LANES), F32), *extra(2), pltpu.SemaphoreType.DMA((3,))],
        connectivity, wave_block, mass_scale.reshape(owned // LANES, LANES),
    )
    ghost = passed_along(face, "cells", 1)
    slots_mid, wave_mid, mass_mid, kinetic, coefficient = call(
        lambda *refs: gather_rest_kernel(vectors, groups, *refs),
        "gather_rest",
        (
            shape(len(MID_PLAN), LANES, kind=I32), rows(75), lines(75), lines(8), lines(125),
        ),
        "vvhhs",
        [pltpu.VMEM((1, LANES), I32), *extra(4), pltpu.SemaphoreType.DMA((2,))],
        table, conn, potential, levels.reshape(1, LANES), live_cells,
    )
    values, wave_low, mass_low, low, top, face_down, face_up = call(
        lambda *refs: first_faces_kernel(vectors, *refs),
        "first_faces",
        (rows(125), rows(25), lines(25), rows(25), rows(25), packed, packed),
        "vvvvvvv",
        [],
        wave_mid, wave_top, mass_mid, mass_top, ghost, kinetic, coefficient,
    )
    above = passed_along(face_down, "cells", -1)
    below = passed_along(face_up, "cells", 1)
    mid = call(
        lambda *refs: rest_kernel(vectors, *refs), "first_rest", rows(75), "vvv", [],
        values, kinetic, coefficient,
    )
    values, base_mid, base_top, low, face_down = call(
        lambda *refs: second_faces_kernel(vectors, *refs),
        "second_faces",
        (rows(125), rows(75), rows(25), rows(25), packed),
        "v" * 13 + "ss",
        [],
        low, mid, top, wave_low, wave_mid, wave_top, mass_low, mass_mid, mass_top,
        above, below, kinetic, coefficient, center, halfwidth,
    )
    above = passed_along(face_down, "cells", -1)
    before, done_top, alone, *earlier = call(
        lambda *refs: second_rest_kernel(vectors, *refs),
        "second_rest",
        (
            shape(table_rows, 256), rows(25), shape(vectors, owned, kind=BF16),
            *[shape(earlier_vectors.shape[0] // BLOCKS, owned // parts, kind=BF16)] * BLOCKS,
        ),
        "v" * 9 + "hhss",
        [scratch_rows(75), scratch_rows(25), wave_scratch, pltpu.SemaphoreType.DMA((1 + BLOCKS,))],
        values, kinetic, coefficient, low, mass_mid, mass_top, base_mid, base_top, slots_mid,
        wave_block, earlier_vectors, center, halfwidth,
    )
    pieces = call(
        lambda *refs: scatter_top_kernel(vectors, *refs),
        "scatter_top",
        (shape(vectors, owned // parts, kind=BF16),) * parts,
        "vvvvvvs",
        [pltpu.VMEM((parts, vectors, owned // parts), BF16), pltpu.VMEM((table_rows, 256), F32)],
        slots_top, before, done_top, mass_top, above, alone, halfwidth,
    )
    pieces = list(pieces)
    for away in sorted(range(1, parts), key=lambda k: -min(k, parts - k)):
        pieces[away] = lax.ppermute(pieces[away], "vecs", turn(away))
    total_vectors = parts * vectors
    share = earlier_vectors.shape[0] // devices
    half, peers = share // 2, devices // cores
    pair = [(i, i ^ 1) for i in range(cells)]
    same_core = [
        [(cores * block + k) * parts + part for block in range(cells // cores) for part in range(parts)]
        for k in range(cores)
    ]
    sent = shape(peers, half, 2 * total_vectors)
    quarter = call(
        lambda *refs: gather_pieces_kernel(parts, *refs),
        "gather_pieces",
        shape(total_vectors, owned // parts, kind=BF16),
        "v" * parts, [], *pieces,
    )
    send, keep = [
        call(
            lambda *refs, other=other: project_kernel(cores, parts, share, other, *refs),
            "project_other" if other else "project_own",
            sent, "v" * (1 + BLOCKS), [], quarter, *earlier,
        )
        for other in (True, False)
    ]
    shares = call(
        pair_sum_kernel, "pair_sum", shape(*sent.shape, kind=BF16), "vv", [],
        keep, lax.ppermute(send, "cells", pair),
    )
    shares = lax.all_to_all(
        shares, AXES, split_axis=0, concat_axis=0, tiled=True, axis_index_groups=same_core
    )
    own_rows, mine = call(
        own_rows_kernel,
        "own_rows",
        (shape(share, total_vectors), shape(peers, half, 2 * total_vectors, kind=BF16)),
        "v", [], shares,
    )
    mine = lax.all_to_all(
        mine, AXES, split_axis=0, concat_axis=0, tiled=True, axis_index_groups=same_core
    )
    theirs = lax.ppermute(mine, "cells", pair)
    filtered = quarter
    for other, spread in ((False, mine), (True, theirs)):
        filtered = call(
            lambda *refs, other=other: filter_kernel(cores, parts, share, other, *refs),
            "filter_other" if other else "filter_own",
            shape(total_vectors, owned // parts),
            "vv" + "v" * BLOCKS,
            [pltpu.VMEM((peers * share, total_vectors), BF16)],
            spread, filtered, *earlier,
        )
    return (filtered, own_rows)


def solution(mesh):
    in_specs = (
        P("vecs", "cells"),
        P(None, "cells"),
        P("cells"),
        P("cells"),
        P("cells"),
        P(None, "cells"),
        P("cells"),
        P(),
        P(),
        P(None, AXES),
    )
    out_specs = (P(None, AXES), P(AXES, None))
    return jax.shard_map(
        per_device, mesh=mesh, in_specs=in_specs, out_specs=out_specs, check_vma=False
    )
```
